32 devices in a mesh: dp: 4 (over y, x), seq: 8 (over z, core).
Axes of the slice: x: 2, y: 2, z: 4, core: 2. Of those that a mesh axis runs over, the one named last changes fastest.
Arguments:
- tokens: float32 [4, 1024, 1024], P('dp', 'seq'), may hold values from -6 to 6
- cotangent: float32 [4, 1024, 1024], P('dp', 'seq'), may hold values from -6 to 6
- doc_ids: int32 [4, 1024], P('dp'), may hold values from 0 to 1, never falling along the last dimension, each value on 1 to 768 neighbouring positions
- in_weight: float32 [1024, 4384], P(('dp', 'seq')), may hold values from -0.1875 to 0.1875
- out_weight: float32 [1024, 2048], P(('dp', 'seq')), may hold values from -0.125 to 0.125
- in_m: float32 [1024, 4384], P(('dp', 'seq')), may hold values from -30 to 30
- in_v: float32 [1024, 4384], P(('dp', 'seq')), may hold values from 1 to 1000
- out_m: float32 [1024, 2048], P(('dp', 'seq')), may hold values from -30 to 30
- out_v: float32 [1024, 2048], P(('dp', 'seq')), may hold values from 1 to 1000
- vec_params: float32 [14688], replicated, as said below
- vec_m: float32 [14688], replicated, may hold values from -30 to 30
- vec_v: float32 [14688], replicated, may hold values from 1 to 1000
Outputs:
- activations: float32 [4, 1024, 1024], P('dp', 'seq')
- input_grad: float32 [4, 1024, 1024], P('dp', 'seq')
- in_grad: float32 [1024, 4384], P(('dp', 'seq'))
- out_grad: float32 [1024, 2048], P(('dp', 'seq'))
- vec_grad: float32 [14688], replicated
- in_new: float32 [1024, 4384], P(('dp', 'seq'))
- out_new: float32 [1024, 2048], P(('dp', 'seq'))
- vec_new: float32 [14688], replicated
- in_m_new: float32 [1024, 4384], P(('dp', 'seq'))
- in_v_new: float32 [1024, 4384], P(('dp', 'seq'))
- out_m_new: float32 [1024, 2048], P(('dp', 'seq'))
- out_v_new: float32 [1024, 2048], P(('dp', 'seq'))
- vec_m_new: float32 [14688], replicated
- vec_v_new: float32 [14688], replicated
The draws below stay inside these ranges and needn't reach their ends.
Inputs may be any that keep to these rules, and one draw needn't show every extreme that they name: `doc_ids`: each row holds document 0 and then document 1, each of one or more positions, none longer than 768. `vec_params`: norm_gain and gate_gain lie in 0.7 to 1.3, skip_gain in 0.5 to 1.5, step_bias in -1 to 1, log_rate in -12 to -3.
All inputs are finite; a program needn't handle non-finite values.
Results may differ from the reference program's by a relative error of at most 0.015.
Values may be sent and summed in bfloat16 or wider, within the bound.
A program may use at most 192 MiB of HBM per device.

```python
import math
import jax
import jax.numpy as jnp
import numpy as np
from jax import lax

D = 1024
DI = 2048
H = 32
P_SIZE = 64
N = 128
KW = 4
STRETCH = 256
STEP = 10
SEQLEN = 1024
SEQS = 4
CONV = 2304
PROJ = 4384
VEC = 14688


def draw_vec_params(key, part):
    subkeys = jax.random.split(key, 7)
    norm_gain = 1.0 + 0.3 * jax.random.uniform(subkeys[0], (D,), jnp.float32, -1.0, 1.0)
    gate_gain = 1.0 + 0.3 * jax.random.uniform(subkeys[1], (DI,), jnp.float32, -1.0, 1.0)
    conv_kernel = 0.5 * jnp.clip(jax.random.normal(subkeys[2], (KW * CONV,), jnp.float32), -4.0, 4.0)
    conv_bias = 0.5 * jnp.clip(jax.random.normal(subkeys[3], (CONV,), jnp.float32), -4.0, 4.0)
    step_bias = jax.random.uniform(subkeys[4], (H,), jnp.float32, -1.0, 1.0)
    log_rate = jax.random.uniform(subkeys[5], (H,), jnp.float32, -10.5, -3.0)
    skip_gain = jax.random.uniform(subkeys[6], (H,), jnp.float32, 0.5, 1.5)
    return jnp.concatenate([norm_gain, gate_gain, conv_kernel, conv_bias, step_bias, log_rate, skip_gain])


def levels(key, shape, cuts, low, largest):
    factor_of = 1.0
    for position, blocks in cuts:
        heights = jax.random.uniform(jax.random.fold_in(jax.random.fold_in(key, 6), position), (blocks,), jnp.float32, low / len(cuts), largest / len(cuts))
        factor_of = factor_of * jnp.repeat(jnp.exp(heights), shape[position] // blocks).reshape((-1,) + (1,) * (len(shape) - 1 - position))
    return factor_of


def profile(amount, total, limit, lean):
    loads = [(1 << 20) // math.isqrt(rank ** lean) + 1 for rank in range(2, amount + 1)]
    spare, given = total - limit - (amount - 1), [1] * (amount - 1)
    while spare > 0:
        movable = [i for i in range(amount - 1) if given[i] < limit]
        whole, budget = sum([loads[i] for i in movable]), spare
        for i in movable:
            extra = min(limit - given[i], max(1, budget * loads[i] // whole), spare)
            given[i] = given[i] + extra
            spare = spare - extra
    return np.array([limit] + given)


def ragged(rng, count, total, most, slope):
    if count == 2:
        one = jax.random.randint(rng, (), max(1, total - most), min(most, total - 1) + 1)
        return jnp.stack([one, total - one])
    tallies = jnp.asarray(profile(count, total, most, slope), jnp.int32)
    couples = (count - 1) // 2
    source_of, taker = tallies[1:1 + 2 * couples:2], tallies[2:2 + 2 * couples:2]
    margin = jnp.minimum(source_of - 1, most - taker)
    moved = jax.random.randint(jax.random.fold_in(rng, 1), (couples,), 0, 1 << 20) % (margin + 1)
    tallies = tallies.at[1:1 + 2 * couples:2].set(source_of - moved).at[2:2 + 2 * couples:2].set(taker + moved)
    return tallies[jax.random.permutation(jax.random.fold_in(rng, 2), count)]


def scatter_about(rng, shape, deviation, limit, cuts=(), held_as=jnp.bfloat16):
    array = jax.random.normal(rng, shape, jnp.float32) * deviation
    if len(cuts) > 0:
        array = levels(rng, shape, cuts, -0.22, 0.18) * array
    return jnp.clip(array, min=-limit, max=limit).astype(held_as)


def setup_inputs(seed: int = 0) -> dict:
    streams_of = jax.random.split(jax.random.key(seed), 13)
    tokens = scatter_about(streams_of[0], (SEQS, SEQLEN, D), 1.0, 6.0, ((0, 4), (1, 8)), jnp.float32)
    cotangent = scatter_about(streams_of[1], (SEQS, SEQLEN, D), 1.0, 6.0, ((0, 4), (1, 8)), jnp.float32)
    doc_ids = jax.vmap(lambda own: jnp.searchsorted(jnp.cumsum(ragged(own, 2, SEQLEN, SEQLEN - SEQLEN // 4, 2)), jnp.arange(SEQLEN), side="right"))(jax.random.split(streams_of[2], SEQS)).reshape((SEQS, SEQLEN)).astype(jnp.int32)
    in_weight = scatter_about(streams_of[3], (D, PROJ), D ** -0.5, 0.1875, ((0, 32),), jnp.float32)
    out_weight = scatter_about(streams_of[4], (D, DI), DI ** -0.5, 0.125, ((0, 32),), jnp.float32)
    in_m = scatter_about(streams_of[5], (D, PROJ), 5.0, 30.0, ((0, 32),), jnp.float32)
    in_v = jnp.clip(jnp.exp(math.log(1000.0) - 6.9077553 * jax.random.uniform(streams_of[6], (D, PROJ), jnp.float32) ** levels(streams_of[6], (D, PROJ), ((0, 32),), -0.2, 0.2)), 1.0, 1000.0)
    out_m = scatter_about(streams_of[7], (D, DI), 5.0, 30.0, ((0, 32),), jnp.float32)
    out_v = jnp.clip(jnp.exp(math.log(1000.0) - 6.9077553 * jax.random.uniform(streams_of[8], (D, DI), jnp.float32) ** levels(streams_of[8], (D, DI), ((0, 32),), -0.2, 0.2)), 1.0, 1000.0)
    vec_params = draw_vec_params(jax.random.fold_in(streams_of[12], 71), 0)
    vec_m = scatter_about(streams_of[10], (VEC,), 5.0, 30.0, (), jnp.float32)
    vec_v = jnp.clip(jnp.exp(jax.random.uniform(streams_of[11], (VEC,), jnp.float32, math.log(1.0), math.log(1000.0))), 1.0, 1000.0)
    return {"tokens": tokens, "cotangent": cotangent, "doc_ids": doc_ids, "in_weight": in_weight, "out_weight": out_weight, "in_m": in_m, "in_v": in_v, "out_m": out_m, "out_v": out_v, "vec_params": vec_params, "vec_m": vec_m, "vec_v": vec_v}


norm_eps = 1e-05
beta_one = 0.9
beta_two = 0.95
learn_rate = 0.03
decay_rate = 0.1
adam_eps = 1e-08
top_precision = lax.Precision.HIGHEST

def unpack(vector):
    cursor = D + DI
    norm_gain = vector[:D]
    gate_gain = vector[D:cursor]
    conv_kernel = vector[cursor:cursor + KW * CONV].reshape(KW, CONV)
    cursor = cursor + KW * CONV
    conv_bias = vector[cursor:cursor + CONV]
    cursor = cursor + CONV
    step_bias = vector[cursor:cursor + H]
    log_rate = vector[cursor + H:cursor + 2 * H]
    skip_gain = vector[cursor + 2 * H:cursor + 3 * H]
    return (norm_gain, gate_gain, conv_kernel, conv_bias, step_bias, log_rate, skip_gain)

def repack(norm_gain, gate_gain, conv_kernel, conv_bias, step_bias, log_rate, skip_gain):
    return jnp.concatenate([norm_gain, gate_gain, conv_kernel.reshape(-1), conv_bias, step_bias, log_rate, skip_gain])

def input_norm(inputs, gain):
    scale = lax.rsqrt(lax.optimization_barrier(jnp.mean(inputs * inputs, axis=-1, keepdims=True)) + norm_eps)
    return inputs * scale * gain[None, :]

def gate_norm(ssd_out, gate_in, gain):
    mixed = ssd_out * jax.nn.silu(gate_in)
    scale = lax.rsqrt(lax.optimization_barrier(jnp.mean(mixed * mixed, axis=-1, keepdims=True)) + norm_eps)
    return mixed * scale * gain[None, :]

def conv_silu(padded, conv_kernel, conv_bias, ext_ids):
    length = padded.shape[0] - (KW - 1)
    own_ids = ext_ids[KW - 1:]
    total = jnp.zeros((length, padded.shape[1]), jnp.float32) + conv_bias[None, :]
    for offset in range(KW):
        valid = (ext_ids[offset:offset + length] == own_ids).astype(jnp.float32)
        total = total + conv_kernel[offset][None, :] * padded[offset:offset + length] * valid[:, None]
    return jax.nn.silu(total)

def rates(step_raw, step_bias, log_rate):
    step_size = jax.nn.softplus(step_raw + step_bias[None, :])
    log_decay = -jnp.exp(log_rate)[None, :] * step_size
    return (step_size, log_decay)

def ssd_block(state, pieces):
    values, input_map, output_map, step_size, log_decay, block_ids, prior_id = pieces
    length = values.shape[0]
    cumulative = jnp.cumsum(log_decay, axis=0)
    rows_index = lax.broadcasted_iota(jnp.int32, (length, length), 0)
    cols_index = lax.broadcasted_iota(jnp.int32, (length, length), 1)
    related = (block_ids[:, None] == block_ids[None, :]) & (rows_index >= cols_index)
    spans = cumulative.T[:, :, None] - cumulative.T[:, None, :]
    decays = jnp.where(related[None], jnp.exp(jnp.where(related[None], spans, 0.0)), 0.0)
    scores = jnp.dot(output_map, input_map.T, precision=top_precision)
    mixing = decays * scores[None] * step_size.T[:, None, :]
    inside = jnp.einsum('hij,jhp->ihp', mixing, values, precision=top_precision)
    carried = (block_ids == prior_id).astype(jnp.float32)
    reach = carried[:, None] * jnp.exp(cumulative)
    entering = jnp.einsum('hpn,in->ihp', state, output_map, precision=top_precision) * reach[:, :, None]
    ending = (block_ids == block_ids[-1]).astype(jnp.float32)
    tail_weight = ending[:, None] * jnp.exp(cumulative[-1][None, :] - cumulative) * step_size
    new_state = state * reach[-1][:, None, None] + jnp.einsum('jh,jhp,jn->hpn', tail_weight, values, input_map, precision=top_precision)
    return (new_state, inside + entering)

def ssd_run(mixed_in, step_size, log_decay, skip_gain, row_ids, prior_id, state, block):
    length = mixed_in.shape[0]
    blocks = length // block
    values = mixed_in[:, :DI].reshape(length, H, P_SIZE)
    input_map = mixed_in[:, DI:DI + N]
    output_map = mixed_in[:, DI + N:]
    shifted = jnp.concatenate([jnp.reshape(prior_id, (1,)).astype(jnp.int32), row_ids[:-1].astype(jnp.int32)])
    priors = shifted.reshape(blocks, block)[:, 0]
    pieces = (values.reshape(blocks, block, H, P_SIZE), input_map.reshape(blocks, block, N), output_map.reshape(blocks, block, N), step_size.reshape(blocks, block, H), log_decay.reshape(blocks, block, H), row_ids.reshape(blocks, block), priors)
    final, outputs = lax.scan(ssd_block, state, pieces)
    result = outputs.reshape(length, H, P_SIZE) + skip_gain[None, :, None] * values
    return (result.reshape(length, DI), final)

def adamw_update(param, grad, first, second):
    first_new = beta_one * first + (1.0 - beta_one) * grad
    second_new = beta_two * second + (1.0 - beta_two) * grad * grad
    corrected = first_new / (1.0 - beta_one ** STEP)
    scaled = jnp.sqrt(second_new / (1.0 - beta_two ** STEP)) + adam_eps
    return (param * (1.0 - learn_rate * decay_rate) - learn_rate * corrected / scaled, first_new, second_new)

def reference(tokens, cotangent, doc_ids, in_weight, out_weight, in_m, in_v, out_m, out_v, vec_params, vec_m, vec_v):
    in_work = in_weight.astype(jnp.bfloat16)
    out_work = out_weight.astype(jnp.bfloat16)
    norm_gain, gate_gain, conv_kernel, conv_bias, step_bias, log_rate, skip_gain = unpack(vec_params)
    block = min(STRETCH, SEQLEN)

    def one_row(totals, row):
        inputs, upstream_f, row_ids = row
        ext_ids = jnp.concatenate([jnp.full((KW - 1,), -1, jnp.int32), row_ids.astype(jnp.int32)])
        normed = input_norm(inputs, norm_gain).astype(jnp.bfloat16)
        projected = jnp.dot(normed, in_work, preferred_element_type=jnp.float32)
        gate_in = projected[:, :DI]
        conv_in = projected[:, DI:DI + CONV].astype(jnp.bfloat16)
        step_raw = projected[:, DI + CONV:]
        padded = jnp.concatenate([jnp.zeros((KW - 1, CONV), jnp.float32), lax.optimization_barrier(conv_in).astype(jnp.float32)])
        mixed_in = lax.optimization_barrier(conv_silu(padded, conv_kernel, conv_bias, ext_ids).astype(jnp.bfloat16)).astype(jnp.float32)

        def ssd_piece(mixed, raw, bias_in, rate_in, skip_in):
            step_size, log_decay = rates(raw, bias_in, rate_in)
            return ssd_run(mixed, step_size, log_decay, skip_in, row_ids, jnp.int32(-1), jnp.zeros((H, P_SIZE, N), jnp.float32), block)[0]
        ssd_out, ssd_back = jax.vjp(ssd_piece, mixed_in, step_raw, step_bias, log_rate, skip_gain)
        gated, gate_back = jax.vjp(gate_norm, ssd_out, gate_in, gate_gain)
        normed_out = gated.astype(jnp.bfloat16)
        outputs = inputs + jnp.dot(normed_out, out_work.T, preferred_element_type=jnp.float32)
        upstream = upstream_f.astype(jnp.bfloat16)
        grad_out_w = jnp.dot(upstream.T, normed_out, preferred_element_type=jnp.float32)
        grad_gated = jnp.dot(upstream, out_work, preferred_element_type=jnp.float32)
        grad_ssd, grad_gate_in, grad_gate_gain = gate_back(grad_gated)
        grad_mixed, grad_raw, grad_bias, grad_rate, grad_skip = ssd_back(grad_ssd)
        _, conv_back = jax.vjp(lambda values, kernel, constant: conv_silu(values, kernel, constant, ext_ids), padded, conv_kernel, conv_bias)
        grad_padded, grad_kernel, grad_cbias = conv_back(grad_mixed)
        grad_proj = jnp.concatenate([grad_gate_in, grad_padded[KW - 1:], grad_raw], axis=1).astype(jnp.bfloat16)
        grad_in_w = jnp.dot(normed.T, grad_proj, preferred_element_type=jnp.float32)
        grad_normed = jnp.dot(grad_proj, in_work.T, preferred_element_type=jnp.float32)
        _, norm_back = jax.vjp(input_norm, inputs, norm_gain)
        grad_inputs, grad_norm_gain = norm_back(grad_normed)
        vector = repack(grad_norm_gain, grad_gate_gain, grad_kernel, grad_cbias, grad_bias, grad_rate, grad_skip)
        totals = (totals[0] + grad_in_w, totals[1] + grad_out_w, totals[2] + vector)
        return (totals, (outputs, upstream_f + grad_inputs))
    start_totals = (jnp.zeros((D, PROJ), jnp.float32), jnp.zeros((D, DI), jnp.float32), jnp.zeros((VEC,), jnp.float32))
    totals, (activations, input_grad) = lax.scan(one_row, start_totals, (tokens, cotangent, doc_ids))
    in_grad, out_grad, vec_grad = totals
    in_new, in_m_new, in_v_new = adamw_update(in_weight, in_grad, in_m, in_v)
    out_new, out_m_new, out_v_new = adamw_update(out_weight, out_grad, out_m, out_v)
    vec_new, vec_m_new, vec_v_new = adamw_update(vec_params, vec_grad, vec_m, vec_v)
    return (activations, input_grad, in_grad, out_grad, vec_grad, in_new, out_new, vec_new, in_m_new, in_v_new, out_m_new, out_v_new, vec_m_new, vec_v_new)
```

```python
import jax
import jax.numpy as jnp
from jax import lax
from jax.experimental import pallas as pl
from jax.experimental.pallas import tpu as pltpu
from jax.sharding import PartitionSpec as P

D = 1024
DI = 2048
H = 32
P_SIZE = 64
N = 128
KW = 4
STRETCH = 256
STEP = 10
CONV = 2304


norm_eps = 1e-05
beta_one = 0.9
beta_two = 0.95
learn_rate = 0.03
decay_rate = 0.1
adam_eps = 1e-08
top_precision = lax.Precision.HIGHEST


def unpack(vector):
    cursor = D + DI
    norm_gain = vector[:D]
    gate_gain = vector[D:cursor]
    conv_kernel = vector[cursor : cursor + KW * CONV].reshape(KW, CONV)
    cursor = cursor + KW * CONV
    conv_bias = vector[cursor : cursor + CONV]
    cursor = cursor + CONV
    step_bias = vector[cursor : cursor + H]
    log_rate = vector[cursor + H : cursor + 2 * H]
    skip_gain = vector[cursor + 2 * H : cursor + 3 * H]
    return (norm_gain, gate_gain, conv_kernel, conv_bias, step_bias, log_rate, skip_gain)


def input_norm(inputs, gain):
    scale = lax.rsqrt(jnp.mean(inputs * inputs, axis=-1, keepdims=True) + norm_eps)
    return inputs * scale * gain[None, :]


def adamw_update(param, grad, first, second):
    first_new = beta_one * first + (1.0 - beta_one) * grad
    second_new = beta_two * second + (1.0 - beta_two) * grad * grad
    corrected = first_new / (1.0 - beta_one**STEP)
    scaled = jnp.sqrt(second_new / (1.0 - beta_two**STEP)) + adam_eps
    return (
        param * (1.0 - learn_rate * decay_rate) - learn_rate * corrected / scaled,
        first_new,
        second_new,
    )


CHUNK = 128
LANES = 128
bf16 = jnp.bfloat16
f32 = jnp.float32


def contract(a, b, left, right):
    return lax.dot_general(a, b, (((left,), (right,)), ((), ())), preferred_element_type=f32)


def spread_heads(table, heads, length):
    return jnp.concatenate(
        [jnp.broadcast_to(table[:, k : k + 1], (length, P_SIZE)) for k in range(heads)], axis=1
    )


def head_slice(block, k):
    return block[:, k * P_SIZE : (k + 1) * P_SIZE]


def chunk_terms(mixed_ref, raw_ref, meta_ref, ids_ref, small_ref, width):
    length = raw_ref.shape[0]
    values = mixed_ref[:, :width].astype(f32)
    input_map = mixed_ref[:, width : width + N]
    output_map = mixed_ref[:, width + N :]
    shifted_raw = raw_ref[...] + small_ref[0:1, :]
    step_size = jnp.maximum(shifted_raw, 0.0) + jnp.log1p(jnp.exp(-jnp.abs(shifted_raw)))
    rate = -jnp.exp(small_ref[1:2, :])
    log_decay = rate * step_size
    rows_index = lax.broadcasted_iota(jnp.int32, (length, length), 0)
    cols_index = lax.broadcasted_iota(jnp.int32, (length, length), 1)
    lower = rows_index >= cols_index
    cumulative = jnp.dot(
        lower.astype(f32), log_decay, precision=top_precision, preferred_element_type=f32
    )
    flipped = cumulative.T
    same = meta_ref[:, 0:1] == ids_ref[...]
    related = same & lower
    reach = meta_ref[:, 1:2] * jnp.exp(cumulative)
    tail = meta_ref[:, 2:3] * jnp.exp(cumulative[length - 1 :, :] - cumulative)
    scores = contract(output_map, input_map, 1, 1)

    def decay_of(k):
        spans = cumulative[:, k : k + 1] - flipped[k : k + 1, :]
        return jnp.exp(jnp.where(related, spans, -1e30))

    return (values, input_map, output_map, shifted_raw, step_size, rate, log_decay, same,
            rows_index, cols_index, reach, tail, scores, decay_of)


def position_table(ids, ext_ids):
    length = ids.shape[0]
    chunked = ids.reshape(-1, CHUNK)
    none = jnp.full((1,), -1, jnp.int32)
    prior = jnp.concatenate([none, chunked[:-1, -1]])[:, None]
    following = jnp.concatenate([chunked[1:, 0], none])[:, None]
    last = chunked[:, -1:]
    columns = [chunked, chunked == prior, chunked == last, chunked == following]
    columns = [column.astype(f32).reshape(-1) for column in columns]
    valid = [(ext_ids[offset : offset + length] == ids).astype(f32) for offset in range(KW - 1)]
    return jnp.pad(jnp.stack(columns + valid + [jnp.ones_like(columns[0])], axis=1), ((0, 8), (0, 0)))


MESH = pl.DeviceIdType.MESH
in_vmem = pl.BlockSpec(memory_space=pltpu.VMEM)


def beyond(axis, distance):
    count = lax.axis_size(axis)
    return lax.rem(lax.axis_index(axis) + distance + count, count)


def push(source, target, send_sem, recv_sem, axis, peer):
    return pltpu.make_async_remote_copy(
        src_ref=source, dst_ref=target, send_sem=send_sem, recv_sem=recv_sem,
        device_id={axis: peer}, device_id_type=MESH,
    )


def greet_all(axes):
    barrier = pltpu.get_barrier_semaphore()
    total = 0
    for axis in axes:
        for step in range(1, lax.axis_size(axis)):
            pl.semaphore_signal(barrier, inc=1, device_id={axis: beyond(axis, step)}, device_id_type=MESH)
            total += 1
    return lambda: pl.semaphore_wait(barrier, total)


def row_gather(seq_count, rows, right_send, right_recv, left_send, left_recv, core_send, core_recv):
    here = lax.axis_index("seq")
    chips = seq_count // 2
    chip, core = here // 2, lax.rem(here, 2)
    partner = here + 1 - 2 * core

    def right(k, peer):
        slot = here - 2 * (k - 1)
        return push(rows.at[slot], rows.at[slot], right_send.at[k], right_recv.at[k], "seq", peer)

    def left(k, peer):
        slot = here + 2 * (k - 1)
        return push(rows.at[slot], rows.at[slot], left_send.at[k], left_recv.at[k], "seq", peer)

    def across(q, slot):
        return push(rows.at[slot], rows.at[slot], core_send.at[q], core_recv.at[q], "seq", partner)

    def sends_right(k):
        return (chip < chips - 1) & (chip >= k - 1)

    def sends_left(k):
        return (chip > 0) & (chip + k <= chips)

    def send(k):
        if k < chips:
            @pl.when(sends_right(k))
            def _():
                right(k, here + 2).start()

            @pl.when(sends_left(k))
            def _():
                left(k, here - 2).start()

    def begin():
        send(1)
        across(chip, here).start()

    def stage(k):
        @pl.when(chip >= k)
        def _():
            slot = here - 2 * k
            push(rows.at[slot], rows.at[slot], right_send.at[k], right_recv.at[k], "seq", partner).wait_recv()

        @pl.when(chip + k < chips)
        def _():
            slot = here + 2 * k
            push(rows.at[slot], rows.at[slot], left_send.at[k], left_recv.at[k], "seq", partner).wait_recv()

        send(k + 1)

        @pl.when(chip >= k)
        def _():
            across(chip - k, here - 2 * k).start()

        @pl.when(chip + k < chips)
        def _():
            across(chip + k, here + 2 * k).start()

    def finish():
        for q in range(chips):
            across(q, 2 * q + 1 - core).wait_recv()
            across(q, 2 * q + core).wait_send()
        for k in range(1, chips):
            @pl.when(sends_right(k))
            def _(k=k):
                right(k, here + 2).wait_send()

            @pl.when(sends_left(k))
            def _(k=k):
                left(k, here - 2).wait_send()

    return begin, stage, finish


def row_scatter(seq_count, total, from_left, from_right, to_right, to_left, right_send, right_recv, left_send, left_recv):
    here = lax.axis_index("seq")
    chips = seq_count // 2
    chip = here // 2

    def right(source, q):
        return push(source.at[q], from_left.at[q], right_send.at[q], right_recv.at[q], "seq", here + 2)

    def left(source, q):
        return push(source.at[q], from_right.at[q], left_send.at[q], left_recv.at[q], "seq", here - 2)

    def begin():
        @pl.when(chip == 0)
        def _():
            for q in range(chips - 1, 0, -1):
                right(total, q).start()

        @pl.when(chip == chips - 1)
        def _():
            for q in range(chips - 1):
                left(total, q).start()

    def slot(t):
        for i in range(chips - 1):
            z = t - i
            q = chips - 1 - i
            if 1 <= z < q:
                @pl.when(chip == z)
                def _(q=q):
                    right(to_right, q).wait_recv()
                    to_right[q] = (total[q].astype(f32) + from_left[q].astype(f32)).astype(bf16)
                    right(to_right, q).start()

                @pl.when(chip == chips - 1 - z)
                def _(q=chips - 1 - q):
                    left(to_left, q).wait_recv()
                    to_left[q] = (total[q].astype(f32) + from_right[q].astype(f32)).astype(bf16)
                    left(to_left, q).start()

    def finish(acc):
        acc[...] = total[chip].astype(f32)

        @pl.when(chip > 0)
        def _():
            right(to_right, chip).wait_recv()
            acc[...] += from_left[chip].astype(f32)

        @pl.when(chip < chips - 1)
        def _():
            left(to_left, chip).wait_recv()
            acc[...] += from_right[chip].astype(f32)

        for q in range(chips):
            @pl.when(chip < q)
            def _(q=q):
                right(to_right, q).wait_send()

            @pl.when(chip > q)
            def _(q=q):
                left(to_left, q).wait_send()

    return begin, slot, finish


def scatter_scratch(block, chips):
    sems = pltpu.SemaphoreType.DMA
    return [pltpu.VMEM(block, bf16)] * 4 + [sems((chips,))] * 4


def spread_kernel(seq_count, dp_count, in_ref, last_ref, tok_ref, gain_ref, out, normed, blocks,
                  seq_send, seq_recv, dp_send, dp_recv, right_send, right_recv, left_send, left_recv,
                  core_send, core_recv):
    here, row = lax.axis_index("seq"), lax.axis_index("dp")
    arrive = greet_all(("seq", "dp"))
    width = DI // seq_count
    heads = H // seq_count
    mixed = width + 2 * N
    chips = seq_count // 2
    shared = in_ref[:, 2 * DI : DI + CONV].astype(bf16)
    step_cols = in_ref[:, DI + CONV :].astype(bf16)
    source = lax.broadcasted_iota(jnp.int32, (H, LANES), 0)
    target = lax.broadcasted_iota(jnp.int32, (H, LANES), 1)
    for p in range(seq_count):
        own = slice(p * width, (p + 1) * width)
        blocks[p, :, :width] = in_ref[:, own].astype(bf16)
        blocks[p, :, width : 2 * width] = in_ref[:, DI + p * width : DI + (p + 1) * width].astype(bf16)
        blocks[p, :, 2 * width : width + mixed] = shared
        chosen = ((source == target + p * heads) & (target < heads)).astype(bf16)
        blocks[p, :, width + mixed : width + mixed + LANES] = contract(step_cols, chosen, 1, 0).astype(bf16)
        blocks[p, :, width + mixed + LANES :] = last_ref[:, own].astype(bf16)
    arrive()

    def seq_copy(step, peer, slot):
        return push(blocks.at[peer], out.at[row, slot], seq_send.at[step], seq_recv.at[step], "seq", peer)

    def launch(step, _):
        seq_copy(step, beyond("seq", step), here).start()
        return 0

    lax.fori_loop(1, seq_count, launch, 0)
    out[row, here] = blocks[here]
    normed[here] = input_norm(tok_ref[...], gain_ref[...][0]).astype(bf16)

    begin, stage, finish_rows = row_gather(seq_count, normed, right_send, right_recv, left_send, left_recv, core_send, core_recv)
    quads = dp_count == 4

    def dp_copy(step, hop, from_row, source_ref):
        piece = beyond("seq", -step)
        return push(source_ref, out.at[from_row, piece], dp_send.at[step, hop], dp_recv.at[step, hop], "dp", flip(hop))

    def flip(hop):
        if not quads:
            return beyond("dp", hop)
        bit = hop if hop < 3 else 0
        low, high = lax.rem(row, 2), row // 2
        if bit == 1:
            return 2 * high + 1 - low
        return 2 * (1 - high) + low

    def origin(hop):
        if not quads:
            return beyond("dp", -hop)
        low, high = lax.rem(row, 2), row // 2
        return [row, 2 * high + 1 - low, 2 * (1 - high) + low, 3 - row][hop]

    def spread_own(step, from_blocks=False):
        piece = beyond("seq", -step)
        source_ref = blocks.at[here] if from_blocks else out.at[row, piece]
        for hop in (1, 2) if quads else range(1, dp_count):
            dp_copy(step, hop, row, source_ref).start()

    def relay_copy(step, via):
        piece = beyond("seq", -step)
        from_row = origin(via)
        return push(out.at[from_row, piece], out.at[from_row, piece], dp_send.at[step, 3], dp_recv.at[step, 3],
                    "dp", flip(3 - via))

    def relay(step):
        if not quads:
            return
        piece = beyond("seq", -step)

        for via in (1, 2):
            dp_copy(step, via, origin(via), out.at[row, piece]).wait_recv()

        @pl.when(lax.rem(step, 2) == 0)
        def _():
            relay_copy(step, 1).start()

        @pl.when(lax.rem(step, 2) == 1)
        def _():
            relay_copy(step, 2).start()

    spread_own(0, True)

    begin()

    def forward(step, _):
        seq_copy(step, beyond("seq", step), beyond("seq", -step)).wait_recv()
        spread_own(step)
        relay(step - 1)
        return 0

    lax.fori_loop(1, seq_count, forward, 0)

    for k in range(1, chips):
        stage(k)
        if k == 1:
            relay(seq_count - 1)
    if chips == 1:
        relay(seq_count - 1)

    def finish(step, _):
        piece = beyond("seq", -step)
        for hop in range(1, dp_count):
            if quads and hop < 3:
                dp_copy(step, hop, row, out.at[row, piece]).wait_send()
            else:
                copy = push(out.at[row, piece], out.at[origin(hop), piece], dp_send.at[step, hop],
                            dp_recv.at[step, hop], "dp", flip(hop))
                copy.wait_recv()
                copy.wait_send()

        @pl.when(step > 0)
        def _():
            seq_copy(step, beyond("seq", step), here).wait_send()

        return 0

    lax.fori_loop(0, seq_count, finish, 0)
    finish_rows()


def spread_weights(in_weight, out_weight, inputs, gain):
    seq_count, dp_count = lax.axis_size("seq"), lax.axis_size("dp")
    sems = pltpu.SemaphoreType.DMA
    width = DI // seq_count
    columns = 3 * width + 2 * N + LANES
    block = (seq_count, in_weight.shape[0], columns)
    chips = (seq_count // 2,)
    return pl.pallas_call(
        lambda *refs: spread_kernel(seq_count, dp_count, *refs),
        out_shape=[
            jax.ShapeDtypeStruct((dp_count,) + block, bf16),
            jax.ShapeDtypeStruct((seq_count,) + inputs.shape, bf16),
        ],
        in_specs=[in_vmem] * 4,
        out_specs=[in_vmem] * 2,
        scratch_shapes=[pltpu.VMEM(block, bf16)]
        + [sems((seq_count,))] * 2 + [sems((seq_count, dp_count))] * 2 + [sems(chips)] * 6,
        compiler_params=pltpu.CompilerParams(collective_id=1, has_side_effects=True),
        name="spread_weights",
    )(in_weight, out_weight, inputs, gain[None, :])


def rows_at(index, size):
    return pl.ds(pl.multiple_of(index * size, size), size)


def conv_window(conv_ref, c):
    return conv_ref[pl.ds(pl.multiple_of(c * CHUNK, CHUNK), CHUNK + 8), :]


def conv_before(window, table, kern_ref):
    taps = []
    total = kern_ref[KW : KW + 1, :]
    for k in range(KW):
        tap = window[8 - (KW - 1) + k : 8 - (KW - 1) + k + CHUNK, :]
        if k < KW - 1:
            tap = tap * table[:, 4 + k : 5 + k]
        taps.append(tap)
        total = total + kern_ref[k : k + 1, :] * tap
    return total, taps


def segments(count, parts):
    marks = [count * p // parts for p in range(parts + 1)]
    return list(zip(marks[:-1], marks[1:]))


def forward_kernel(seq_count, normed, weights, cotangent, table_ref, ids_ref, small_ref, kern_ref,
                   gate_ref, conv_ref, raw_ref, mixed_ref, ssd_ref, entry_ref, upstream,
                   state, *sems):
    heads = H // seq_count
    width = heads * P_SIZE
    mixed_width = width + 2 * N
    in_width = width + mixed_width + LANES
    length = normed.shape[0]
    here = lax.axis_index("seq")
    chips = seq_count // 2
    arrive = greet_all(("seq",))
    begin, stage, finish = row_gather(seq_count, upstream, *sems)
    upstream[here] = cotangent[...].astype(bf16)
    conv_ref[0:8, :] = jnp.zeros((8, mixed_width), f32)
    state[...] = jnp.zeros_like(state)
    arrive()
    begin()
    tall = 2 * CHUNK

    def project(i, _):
        out = contract(normed[rows_at(i, tall), :], weights[:, :in_width], 1, 0)
        gate_ref[rows_at(i, tall), :] = out[:, :width]
        conv_ref[pl.ds(pl.multiple_of(i * tall + 8, 8), tall), :] = out[:, width : width + mixed_width].astype(bf16).astype(f32)
        raw_ref[rows_at(i, tall), :] = out[:, width + mixed_width :]
        return 0

    lax.fori_loop(0, length // tall, project, 0)

    def chunk(c, _):
        table = table_ref[rows_at(c, CHUNK), :]
        before, _ = conv_before(conv_window(conv_ref, c), table, kern_ref)
        mixed = (before / (1.0 + jnp.exp(-before))).astype(bf16)
        mixed_ref[rows_at(c, CHUNK), :] = mixed
        (values, input_map, output_map, _, step_size, _, _, _, _, _, reach, tail, scores, decay_of) = (
            chunk_terms(mixed, raw_ref[rows_at(c, CHUNK), :], table, ids_ref[pl.ds(c, 1), :], small_ref, width)
        )
        entry = state[...]
        entry_low = entry.astype(bf16)
        entry_ref[c] = entry_low
        fed = (values * spread_heads(step_size, heads, CHUNK)).astype(bf16)
        inside = []
        for k in range(heads):
            mixing = (scores * decay_of(k)).astype(bf16)
            inside.append(contract(mixing, head_slice(fed, k), 1, 0))
        wide_reach = spread_heads(reach, heads, CHUNK)
        ssd_ref[rows_at(c, CHUNK), :] = jnp.concatenate(inside, axis=1) + wide_reach * contract(output_map, entry_low, 1, 0)
        weighted = (fed.astype(f32) * spread_heads(tail, heads, CHUNK)).astype(bf16)
        state[...] = entry * wide_reach[CHUNK - 1 :, :] + contract(input_map, weighted, 0, 0)
        return 0

    parts = segments(length // CHUNK, chips)
    for k, (low, high) in enumerate(parts):
        lax.fori_loop(low, high, chunk, 0)
        if k + 1 < chips:
            stage(k + 1)
    finish()


def shapes(*pairs):
    return [jax.ShapeDtypeStruct(shape, kind) for shape, kind in pairs]


def call(kernel, name, number, outs, scratch, operands, flops):
    params = dict(has_side_effects=True, collective_id=number, vmem_limit_bytes=60 * 1024 * 1024)
    return pl.pallas_call(
        kernel,
        out_shape=outs,
        in_specs=[in_vmem] * len(operands),
        out_specs=[in_vmem] * len(outs),
        scratch_shapes=scratch,
        compiler_params=pltpu.CompilerParams(**params),
        cost_estimate=pl.CostEstimate(flops=flops, bytes_accessed=8 * 1024 * 1024, transcendentals=0),
        name=name,
    )(*operands)


def forward(normed, weights, cotangent, table, ids, small, kern):
    seq_count = lax.axis_size("seq")
    length = normed.shape[0]
    width = DI // seq_count
    mixed_width = width + 2 * N
    count = length // CHUNK
    sems = pltpu.SemaphoreType.DMA
    outs = shapes(
        ((length, width), f32), ((length + 8, mixed_width), f32), ((length, LANES), f32), ((length, mixed_width), bf16),
        ((length, width), f32), ((count, N, width), bf16), ((seq_count,) + cotangent.shape, bf16),
    )
    scratch = [pltpu.VMEM((N, width), f32)] + [sems((seq_count // 2,))] * 6
    return call(lambda *refs: forward_kernel(seq_count, *refs), "forward", 2, outs, scratch,
                (normed, weights, cotangent, table, ids, small, kern), 2 * length * D * weights.shape[1])


def middle_kernel(seq_count, upstream, weights, ssd_ref, mixed_ref, gate_ref, gain_ref, skip_ref, normed,
                  total, grad_ref, low_ref, early, scale_ref, gain_grad, norm_row,
                  product_ref, gg_ref, part, arrived, theirs, got, out_low, send, recv, stat_send, stat_recv):
    width = DI // seq_count
    here = lax.axis_index("seq")
    chips = seq_count // 2
    core = lax.rem(here, 2)
    partner = here + 1 - 2 * core
    length = upstream.shape[0]
    count = length // CHUNK
    first = weights.shape[1] - width
    tall = 2 * CHUNK
    arrive = greet_all(("seq",))
    part[...] = jnp.zeros_like(part)
    line = lax.broadcasted_iota(jnp.int32, (2 * count, width), 0)

    def forward_part(i, _):
        at = rows_at(i, tall)
        gg = contract(upstream[at, :], weights[:, first:], 1, 0)
        gate_in = gate_ref[at, :]
        gate_act = gate_in / (1.0 + jnp.exp(-gate_in))
        product = (ssd_ref[at, :] + skip_ref[...] * mixed_ref[at, :width].astype(f32)) * gate_act
        product_ref[at, :] = product
        gg_ref[at, :] = gg
        square = product * product
        crossed = gg * gain_ref[...] * product
        sums = part[...]
        for half in range(2):
            rows = slice(half * CHUNK, (half + 1) * CHUNK)
            for offset, value in ((0, square), (count, crossed)):
                chosen = (line == 2 * i + half + offset).astype(f32)
                sums = sums + lax.dot_general(chosen, value[rows], (((1,), (1,)), ((), ())), precision=top_precision, preferred_element_type=f32)
        part[...] = sums
        return 0

    lax.fori_loop(0, length // tall, forward_part, 0)
    arrive()
    copies = [
        push(part, arrived.at[step], stat_send.at[step], stat_recv.at[step], "seq", beyond("seq", step))
        for step in range(1, seq_count)
    ]
    for copy in copies:
        copy.start()
    arrived[0] = part[...]
    long = total.shape[1]

    def term(piece):
        raw_out = (product_ref[rows_at(piece, long), :] * gain_ref[...]).astype(bf16)
        return contract(raw_out, weights[:, first:], 1, 1)

    def exchange(j):
        return push(theirs.at[j], got.at[j], send.at[j], recv.at[j], "seq", partner)

    def give(j, _):
        theirs[j] = term(2 * j + 1 - core).astype(bf16)

        @pl.when(j > 0)
        def _():
            exchange(j - 1).start()

        return 0

    lax.fori_loop(0, chips, give, 0)

    def keep(j, _):
        own = term(2 * j + core)

        @pl.when(j == 0)
        def _():
            exchange(chips - 1).start()

        exchange(j).wait_recv()
        total[j] = (own + got[j].astype(f32)).astype(bf16)
        return 0

    lax.fori_loop(0, chips, keep, 0)
    for copy in copies:
        copy.wait_recv()
    final = arrived[here]
    for origin in range(1, seq_count):
        final = final + arrived[lax.rem(here - origin + seq_count, seq_count)]
    scale = lax.rsqrt(final[:count] / DI + norm_eps)
    pull = scale * scale * scale * final[count:] / DI
    columns = jnp.concatenate([scale, pull], axis=0).T
    lane = lax.broadcasted_iota(jnp.int32, columns.shape, 1)
    scale_ref[...] = jnp.broadcast_to(
        jnp.sum(jnp.where(lane == here, columns, 0.0), axis=1, keepdims=True), scale_ref.shape
    )
    gain_grad[...] = jnp.zeros_like(gain_grad)

    def back(j, _):
        at = rows_at(j, CHUNK)
        own_scale = jnp.sum(jnp.where(lane == j, columns, 0.0), axis=1, keepdims=True)
        own_pull = jnp.sum(jnp.where(lane == j + count, columns, 0.0), axis=1, keepdims=True)
        gate_in = gate_ref[at, :]
        gate_sig = 1.0 / (1.0 + jnp.exp(-gate_in))
        ssd_out = ssd_ref[at, :] + skip_ref[...] * mixed_ref[at, :width].astype(f32)
        product = product_ref[at, :]
        gg = gg_ref[at, :]
        grad_product = gg * gain_ref[...] * own_scale - product * own_pull
        grad_ref[at, :] = grad_product * gate_in * gate_sig
        low_ref[at, :] = (grad_product * ssd_out * (gate_sig * (1.0 + gate_in * (1.0 - gate_sig)))).astype(bf16)
        gain_grad[0:1, :] += jnp.sum(gg * product * own_scale, axis=0, keepdims=True)
        raw_out = (product * gain_ref[...]).astype(bf16).astype(f32)
        out_low[at, :] = (raw_out * own_scale).astype(bf16)
        return 0

    lax.fori_loop(0, count, back, 0)

    def weigh(b, _):
        at = rows_at(b, tall)
        gate_grad = contract(normed[:, at], low_ref[...], 0, 0)
        early[at, :width] = gate_grad.astype(bf16)
        early[at, width:] = contract(upstream[:, at], out_low[...], 0, 0).astype(bf16)
        norm_row[:, at] = row_sums(weights[at, :width].astype(f32) * gate_grad)
        return 0

    lax.fori_loop(0, D // tall, weigh, 0)
    for j in range(chips):
        exchange(j).wait_send()
    for copy in copies:
        copy.wait_send()


def row_sums(matrix):
    ones = jnp.ones((8, matrix.shape[1]), f32)
    return lax.dot_general(ones, matrix, (((1,), (1,)), ((), ())), precision=top_precision, preferred_element_type=f32)


def middle(upstream, weights, ssd, mixed, gate_in, gain, skip, normed):
    seq_count = lax.axis_size("seq")
    length = upstream.shape[0]
    width = DI // seq_count
    chips = seq_count // 2
    count = length // CHUNK
    block = (chips, length // seq_count, D)
    sems = pltpu.SemaphoreType.DMA
    outs = shapes(
        (block, bf16), ((length, width), f32), ((length, width), bf16), ((D, 2 * width), bf16),
        ((length // seq_count, LANES), f32), ((8, width), f32), ((8, D), f32),
    )
    scratch = [
        pltpu.VMEM((length, width), f32), pltpu.VMEM((length, width), f32), pltpu.VMEM((2 * count, CHUNK), f32),
        pltpu.VMEM((seq_count, 2 * count, CHUNK), f32), pltpu.VMEM(block, bf16), pltpu.VMEM(block, bf16),
        pltpu.VMEM((length, width), bf16), sems((chips,)), sems((chips,)), sems((seq_count,)), sems((seq_count,)),
    ]
    return call(lambda *refs: middle_kernel(seq_count, *refs), "middle", 4, outs, scratch,
                (upstream, weights, ssd, mixed, gate_in, gain, skip, normed), 8 * length * D * width)


def backward_kernel(seq_count, dp_count, mixed_ref, raw_ref, table_ref, ids_ref, small_ref, skip_ref, ssd_ref, entry_ref,
                    grad_ref, conv_ref, kern_ref, out_total, early, scale_ref, tok_ref,
                    late_ref, totals_ref, gkern_ref, early_sum, out_ref,
                    later, carry, ahead, acc, early_got, early_send, early_recv, *chain):
    heads = H // seq_count
    width = heads * P_SIZE
    mixed_width = width + 2 * N
    length = raw_ref.shape[0]
    count = length // CHUNK
    chips = seq_count // 2
    row = lax.axis_index("dp")
    arrive = greet_all(("seq", "dp"))
    begin, slot, finish = row_scatter(seq_count, out_total, *chain)
    for ref in (later, carry, ahead, totals_ref, gkern_ref):
        ref[...] = jnp.zeros_like(ref)
    arrive()
    begin()

    def early_copy(hop):
        peer = beyond("dp", hop)
        return push(early.at[peer], early_got.at[hop], early_send.at[hop], early_recv.at[hop], "dp", peer)

    for hop in range(1, dp_count):
        early_copy(hop).start()
    channel = lax.broadcasted_iota(jnp.int32, (width, LANES), 0)
    lane = lax.broadcasted_iota(jnp.int32, (width, LANES), 1)
    member = ((channel >= lane * P_SIZE) & (channel < (lane + 1) * P_SIZE)).astype(f32)

    def per_head(wide):
        return jnp.dot(wide, member, precision=top_precision, preferred_element_type=f32)

    def chunk(turn, _):
        c = count - 1 - turn
        at = rows_at(c, CHUNK)
        table = table_ref[at, :]
        (values, input_map, output_map, shifted_raw, step_size, rate, log_decay, same, rows_index,
         cols_index, reach, tail, scores, decay_of) = chunk_terms(
            mixed_ref[at, :], raw_ref[at, :], table, ids_ref[pl.ds(c, 1), :], small_ref, width
        )
        grad = grad_ref[at, :]
        grad_low = grad.astype(bf16)
        wide_step = spread_heads(step_size, heads, CHUNK)
        wide_reach = spread_heads(reach, heads, CHUNK)
        wide_tail = spread_heads(tail, heads, CHUNK)
        fed = (values * wide_step).astype(bf16)
        fed_full = fed.astype(f32)
        after = later[...]
        after_low = after.astype(bf16)
        grad_scores = jnp.zeros((CHUNK, CHUNK), f32)
        pieces = []
        for k in range(heads):
            decay = decay_of(k)
            mixing = (scores * decay).astype(bf16)
            own_grad = head_slice(grad_low, k)
            grad_scores = grad_scores + contract(own_grad, head_slice(fed, k), 1, 1) * decay
            pieces.append(contract(mixing, own_grad, 0, 0))
        grad_fed = jnp.concatenate(pieces, axis=1) + wide_tail * contract(input_map, after_low, 1, 0)
        reached = (grad * wide_reach).astype(bf16)
        weighted = (fed_full * wide_tail).astype(bf16)
        scores_low = grad_scores.astype(bf16)
        grad_mixed = jnp.concatenate(
            [
                wide_step * grad_fed + skip_ref[...] * grad,
                contract(scores_low, output_map, 0, 0) + contract(weighted, after_low, 1, 1),
                contract(scores_low, input_map, 1, 0) + contract(reached, entry_ref[c], 1, 1),
            ],
            axis=1,
        )
        later[...] = after * wide_reach[CHUNK - 1 :, :] + contract(output_map, reached, 0, 0)
        balance = per_head(grad_low.astype(f32) * ssd_ref[at, :] - fed_full * grad_fed)
        grad_step = per_head(values * grad_fed)
        skip_total = per_head(jnp.broadcast_to(jnp.sum(values * grad, axis=0, keepdims=True), (8, width)))
        following = (same & (rows_index <= cols_index)).astype(f32)
        grad_log = jnp.dot(
            following, balance, precision=top_precision, preferred_element_type=f32
        ) + table[:, 3:4] * carry[0:1, :]
        carry[0:1, :] = grad_log[0:1, :]
        grad_step = grad_step + rate * grad_log
        grad_raw = grad_step * jax.nn.sigmoid(shifted_raw)
        totals_ref[0:1, :] += jnp.sum(grad_raw, axis=0, keepdims=True)
        totals_ref[1:2, :] += jnp.sum(grad_log * log_decay, axis=0, keepdims=True)
        totals_ref[2:3, :] += skip_total[0:1, :]
        before, taps = conv_before(conv_window(conv_ref, c), table, kern_ref)
        sig = 1.0 / (1.0 + jnp.exp(-before))
        grad_before = grad_mixed * (sig * (1.0 + before * (1.0 - sig)))
        for k in range(KW):
            gkern_ref[k : k + 1, :] += jnp.sum(grad_before * taps[k], axis=0, keepdims=True)
        gkern_ref[KW : KW + 1, :] += jnp.sum(grad_before, axis=0, keepdims=True)
        window = jnp.concatenate([grad_before, ahead[...]], axis=0)
        ahead[...] = grad_before[:8, :]
        wide_table = table_ref[pl.ds(pl.multiple_of(c * CHUNK, CHUNK), CHUNK + 8), :]
        grad_conv = kern_ref[KW - 1 : KW, :] * grad_before
        for k in range(KW - 1):
            shift = KW - 1 - k
            masked = window * wide_table[:, 4 + k : 5 + k]
            grad_conv = grad_conv + kern_ref[k : k + 1, :] * masked[shift : shift + CHUNK, :]
        late_ref[at, :mixed_width] = grad_conv.astype(bf16)
        late_ref[at, mixed_width:] = grad_raw.astype(bf16)
        return 0

    parts = segments(count, chips - 1) if chips > 1 else [(0, count)]
    for t, (low, high) in enumerate(parts):
        lax.fori_loop(low, high, chunk, 0)
        if t + 1 < chips - 1:
            slot(t + 1)
    for hop in range(1, dp_count):
        early_copy(hop).wait_recv()

    def combine(piece, _):
        value = early[row, piece].astype(f32)
        for hop in range(1, dp_count):
            value = value + early_got[hop, piece].astype(f32)
        early_sum[piece] = value.astype(bf16)
        return 0

    lax.fori_loop(0, seq_count, combine, 0)
    finish(acc)
    out_ref[...] = tok_ref[...] + acc[...] * scale_ref[:, 0:1]
    for hop in range(1, dp_count):
        early_copy(hop).wait_send()


def backward(mixed, raw, table, ids, small, skip, ssd, entries, grad, conv_in, kern, out_total, early, scale, tokens):
    seq_count, dp_count = lax.axis_size("seq"), lax.axis_size("dp")
    length = raw.shape[0]
    width = DI // seq_count
    mixed_width = width + 2 * N
    sems = pltpu.SemaphoreType.DMA
    outs = shapes(
        ((length, mixed_width + LANES), bf16), ((8, LANES), f32), ((8, mixed_width), f32),
        (early.shape[1:], bf16), (tokens.shape, f32),
    )
    scratch = [
        pltpu.VMEM((N, width), f32), pltpu.VMEM((8, LANES), f32), pltpu.VMEM((8, mixed_width), f32), pltpu.VMEM(tokens.shape, f32),
        pltpu.VMEM(early.shape, bf16), sems((dp_count,)), sems((dp_count,)),
    ] + scatter_scratch(out_total.shape, seq_count // 2)
    return call(lambda *refs: backward_kernel(seq_count, dp_count, *refs), "backward", 5, outs, scratch,
                (mixed, raw, table, ids, small, skip, ssd, entries, grad, conv_in, kern, out_total, early, scale, tokens),
                16 * length * N * width)


def final_kernel(seq_count, dp_count, lines, low_ref, late_ref, weights, normed, early, gain_ref, norm_row, gain_grad,
                 gkern_ref, totals_ref, tok_ref, cot_ref,
                 returned, returned_early, vec_out, in_grad_ref,
                 total, theirs, got_rows, part, got, summed, vec, vec_dp, vec_row, vec_seq, acc,
                 pair_send, pair_recv, dp_send, dp_recv, seq_send, seq_recv, early_send, early_recv,
                 va_send, va_recv, vb_send, vb_recv, vc_send, vc_recv, vd_send, vd_recv, *chain):
    here, row = lax.axis_index("seq"), lax.axis_index("dp")
    heads = H // seq_count
    width = DI // seq_count
    mixed_width = width + 2 * N
    in_width = width + mixed_width + LANES
    chips = seq_count // 2
    core = lax.rem(here, 2)
    partner = here + 1 - 2 * core
    hops = range(1, dp_count)
    steps = range(1, seq_count)
    tall = 2 * CHUNK
    share = part.shape[1]
    begin, slot, finish_rows = row_scatter(seq_count, total, *chain)
    arrive = greet_all(("seq", "dp"))
    arrive()

    def early_copy(step, place):
        piece = beyond("seq", step)
        return push(early.at[piece], returned_early.at[place], early_send.at[step], early_recv.at[step], "seq", piece)

    for step in steps:
        early_copy(step, here).start()
    returned_early[here] = early[here]

    long = total.shape[1]

    def term(piece):
        at = rows_at(piece, long)
        return contract(low_ref[at, :], weights[:, :width], 1, 1) + contract(late_ref[at, :], weights[:, width:in_width], 1, 1)

    def pair(j):
        return push(theirs.at[j], got_rows.at[j], pair_send.at[j], pair_recv.at[j], "seq", partner)

    def give(j, _):
        theirs[j] = term(2 * j + 1 - core).astype(bf16)

        @pl.when(j > 0)
        def _():
            pair(j - 1).start()

        return 0

    lax.fori_loop(0, chips, give, 0)

    def keep(j, _):
        own = term(2 * j + core)

        @pl.when(j == 0)
        def _():
            pair(chips - 1).start()

        pair(j).wait_recv()
        total[j] = (own + got_rows[j].astype(f32)).astype(bf16)
        return 0

    lax.fori_loop(0, chips, keep, 0)
    begin()

    vec[...] = jnp.zeros_like(vec)

    def weigh(b, _):
        at = rows_at(b, tall)
        grads = contract(normed[:, at], late_ref[...], 0, 0)
        for i in range(tall // share):
            part[b * (tall // share) + i] = grads[i * share : (i + 1) * share, :].astype(bf16)
        sums = row_sums(weights[at, width:in_width].astype(f32) * grads)
        sums = (sums + norm_row[:, at]) / gain_ref[:, at]
        for j in range(tall // LANES):
            vec[pl.ds(b * (tall // LANES) + j, 1), :] = sums[0:1, j * LANES : (j + 1) * LANES]
        return 0

    lax.fori_loop(0, D // tall, weigh, 0)

    def write(base, source, line, columns, moving):
        for j in range(columns[0] // LANES, columns[1] // LANES):
            at = base + j - columns[0] // LANES
            if moving:
                at = at + here * (width // LANES)
            vec[pl.ds(at, 1), :] = source[line : line + 1, j * LANES : (j + 1) * LANES]

    base = D // LANES
    write(base, gain_grad, 0, (0, width), True)
    base += DI // LANES
    for k in range(KW + 1):
        write(base, gkern_ref, k, (0, width), True)
        write(base + DI // LANES, gkern_ref, k, (width, mixed_width), False)
        base += CONV // LANES
    source = lax.broadcasted_iota(jnp.int32, (LANES, LANES), 0)
    target = lax.broadcasted_iota(jnp.int32, (LANES, LANES), 1)
    tail = jnp.zeros((8, LANES), f32)
    picked = lax.broadcasted_iota(jnp.int32, (8, LANES), 0)
    sums = totals_ref[...]
    for k in range(3):
        chosen = ((target == source + k * H + here * heads) & (source < heads)).astype(f32)
        tail = tail + jnp.dot(jnp.where(picked == k, sums, 0.0), chosen, precision=top_precision, preferred_element_type=f32)
    vec[base : base + 1, :] = jnp.sum(tail, axis=0, keepdims=True)

    wide = seq_count * lines
    first = [push(vec.at[rows_at(beyond("dp", hop), wide), :], vec_dp.at[hop], va_send.at[hop], va_recv.at[hop], "dp", beyond("dp", hop)) for hop in hops]
    for copy in first:
        copy.start()
    def dp_copy(step, hop):
        piece = beyond("seq", step)
        peer = beyond("dp", hop)
        return push(part.at[peer * seq_count + piece], got.at[hop, piece], dp_send.at[step, hop], dp_recv.at[step, hop], "dp", peer)

    def launch(step, _):
        for hop in hops:
            dp_copy(lax.rem(step, seq_count), hop).start()
        return 0

    lax.fori_loop(1, seq_count + 1, launch, 0)
    for copy in first:
        copy.wait_recv()
    value = vec[rows_at(row, wide), :]
    for hop in hops:
        value = value + vec_dp[hop]
    vec_row[...] = value
    second = [push(vec_row.at[rows_at(beyond("seq", step), lines), :], vec_seq.at[step], vb_send.at[step], vb_recv.at[step], "seq", beyond("seq", step)) for step in steps]
    for copy in second:
        copy.start()
    if chips > 2:
        slot(1)

    def seq_copy(step, place):
        piece = beyond("seq", step)
        return push(summed.at[piece], returned.at[place], seq_send.at[step], seq_recv.at[step], "seq", piece)

    def combined(step):
        piece = beyond("seq", step)
        for hop in hops:
            dp_copy(step, hop).wait_recv()
        value = part[row * seq_count + piece].astype(f32)
        for hop in hops:
            value = value + got[hop, piece].astype(f32)
        return value.astype(bf16)

    def swap(step, _):
        summed[beyond("seq", step)] = combined(step)
        seq_copy(step, here).start()
        return 0

    half = seq_count // 2
    lax.fori_loop(1, half, swap, 0)
    for copy in second:
        copy.wait_recv()
    final = vec_row[rows_at(here, lines), :]
    for step in steps:
        final = final + vec_seq[step]
    spot = row * seq_count + here
    vec_out[rows_at(spot, lines), :] = final

    def third(step, place):
        at = rows_at(row * seq_count + place, lines)
        return push(vec_out.at[rows_at(spot, lines), :], vec_out.at[at, :], vc_send.at[step], vc_recv.at[step], "seq", beyond("seq", step))

    for step in steps:
        third(step, here).start()
    for t in range(2, chips - 1):
        slot(t)
    lax.fori_loop(half, seq_count, swap, 0)
    returned[here] = combined(0)
    for step in steps:
        third(step, beyond("seq", -step)).wait_recv()

    def fourth(hop, place):
        return push(vec_out.at[rows_at(row, wide), :], vec_out.at[rows_at(place, wide), :], vd_send.at[hop], vd_recv.at[hop], "dp", beyond("dp", hop))

    for hop in hops:
        fourth(hop, row).start()
    finish_rows(acc)
    inputs = tok_ref[...]
    scale = lax.rsqrt(jnp.mean(inputs * inputs, axis=-1, keepdims=True) + norm_eps)
    pulled = acc[...] * gain_ref[...]
    dots = jnp.sum(pulled * inputs, axis=-1, keepdims=True)
    in_grad_ref[...] = cot_ref[...] + scale * pulled - inputs * (scale * scale * scale * dots / D)

    def close(step, _):
        seq_copy(step, beyond("seq", -step)).wait_recv()
        seq_copy(step, here).wait_send()
        early_copy(step, beyond("seq", -step)).wait_recv()
        early_copy(step, here).wait_send()
        return 0

    lax.fori_loop(1, seq_count, close, 0)

    def drain(step, _):
        for hop in hops:
            dp_copy(step, hop).wait_send()
        return 0

    lax.fori_loop(0, seq_count, drain, 0)
    for hop in hops:
        fourth(hop, beyond("dp", -hop)).wait_recv()
        fourth(hop, row).wait_send()
    for copy in first + second:
        copy.wait_send()
    for step in steps:
        third(step, here).wait_send()
    for j in range(chips):
        pair(j).wait_send()


def final(low, late, weights, normed, early, gain, norm_row, gain_grad, gkern, totals, tokens, cotangent):
    seq_count, dp_count = lax.axis_size("seq"), lax.axis_size("dp")
    devices = seq_count * dp_count
    chips = seq_count // 2
    vec_size = D + DI + (KW + 1) * CONV + 3 * H
    lines = -(-vec_size // (devices * LANES * 8)) * 8
    share = D // devices
    columns = late.shape[1]
    block = (chips,) + tokens.shape
    sems = pltpu.SemaphoreType.DMA
    outs = shapes(
        ((seq_count, share, columns), bf16), (early.shape, bf16), ((devices * lines, LANES), f32), (tokens.shape, f32)
    )
    scratch = [
        pltpu.VMEM(block, bf16), pltpu.VMEM(block, bf16), pltpu.VMEM(block, bf16), pltpu.VMEM((devices, share, columns), bf16),
        pltpu.VMEM((dp_count, seq_count, share, columns), bf16), pltpu.VMEM((seq_count, share, columns), bf16),
        pltpu.VMEM((devices * lines, LANES), f32), pltpu.VMEM((dp_count, seq_count * lines, LANES), f32),
        pltpu.VMEM((seq_count * lines, LANES), f32), pltpu.VMEM((seq_count, lines, LANES), f32), pltpu.VMEM(tokens.shape, f32),
    ]
    counts = [(chips,)] * 2 + [(seq_count, dp_count)] * 2 + [(seq_count,)] * 4 + [(dp_count,)] * 2 + [(seq_count,)] * 4 + [(dp_count,)] * 2
    scratch += [sems(shape) for shape in counts] + scatter_scratch(block, chips)
    return call(lambda *refs: final_kernel(seq_count, dp_count, lines, *refs), "final", 3, outs, scratch,
                (low, late, weights, normed, early, gain, norm_row, gain_grad, gkern, totals, tokens, cotangent),
                4 * D * D * columns)


def body(tokens, cotangent, doc_ids, in_weight, out_weight, in_m, in_v, out_m, out_v, vec_params, vec_m, vec_v):
    seq_count = lax.axis_size("seq")
    place = lax.axis_index("seq")
    heads = H // seq_count
    width = DI // seq_count
    mixed_width = width + 2 * N
    owner_rows = in_weight.shape[0]
    inputs = tokens[0]
    upstream_f = cotangent[0]
    norm_gain = vec_params[:D]

    weights, normed_all = spread_weights(in_weight, out_weight, inputs, norm_gain)
    weights = weights.reshape(D, -1)
    normed_all = normed_all.reshape(-1, D)
    _, gate_gain, conv_kernel, conv_bias, step_bias, log_rate, skip_gain = unpack(vec_params)
    ids = doc_ids[0]
    ext_ids = jnp.concatenate([jnp.full((KW - 1,), -1, jnp.int32), ids])
    table = position_table(ids, ext_ids)
    ids_rows = ids.astype(f32).reshape(-1, CHUNK)

    def own(vector, size):
        return lax.dynamic_slice_in_dim(vector, place * size, size, vector.ndim - 1)

    own_gain = own(gate_gain, width)[None, :]
    both = jnp.concatenate([conv_kernel, conv_bias[None, :]])
    kern = jnp.pad(jnp.concatenate([own(both[:, :DI], width), both[:, DI:]], axis=1), ((0, 7 - KW), (0, 0)))
    wide_skip = jnp.repeat(own(skip_gain, heads), P_SIZE)[None, :]
    small = jnp.pad(jnp.stack([own(step_bias, heads), own(log_rate, heads)]), ((0, 6), (0, LANES - heads)))

    gate_in, conv_in, raw, mixed, ssd, entries, upstream_all = forward(
        normed_all, weights, upstream_f, table, ids_rows, small, kern
    )
    upstream_all = upstream_all.reshape(-1, D)
    out_total, grad_ssd, gate_low, early, scale, gain_grad, norm_row = middle(
        upstream_all, weights, ssd, mixed, gate_in, own_gain, wide_skip, normed_all
    )
    early = early.reshape(lax.axis_size("dp"), seq_count, owner_rows, -1)
    late, totals, gkern, early, outputs = backward(
        mixed, raw, table, ids_rows, small, wide_skip, ssd, entries, grad_ssd, conv_in, kern, out_total, early, scale, inputs
    )
    returned, returned_early, vec_sum, input_grad = final(
        gate_low, late, weights, normed_all, early, norm_gain[None, :], norm_row, gain_grad, gkern, totals, inputs, upstream_f
    )
    returned = returned.astype(f32)
    returned_early = returned_early.astype(f32)
    vec_grad = vec_sum.reshape(-1)[: vec_params.shape[0]]

    def gathered(array, start, size):
        return array[:, :, start : start + size].transpose(1, 0, 2).reshape(owner_rows, -1)

    in_grad = jnp.concatenate(
        [
            gathered(returned_early, 0, width),
            gathered(returned, 0, width),
            jnp.sum(returned[:, :, width : width + 2 * N], axis=0),
            gathered(returned, mixed_width, heads),
        ],
        axis=1,
    )
    out_grad = gathered(returned_early, width, width)

    in_new, in_m_new, in_v_new = adamw_update(in_weight, in_grad, in_m, in_v)
    out_new, out_m_new, out_v_new = adamw_update(out_weight, out_grad, out_m, out_v)
    vec_new, vec_m_new, vec_v_new = adamw_update(vec_params, vec_grad, vec_m, vec_v)
    return (
        outputs[None],
        input_grad[None],
        in_grad,
        out_grad,
        vec_grad,
        in_new,
        out_new,
        vec_new,
        in_m_new,
        in_v_new,
        out_m_new,
        out_v_new,
        vec_m_new,
        vec_v_new,
    )


def solution(mesh):
    in_specs = (
        P("dp", "seq", None),
        P("dp", "seq", None),
        P("dp", None),
        P(("dp", "seq"), None),
        P(("dp", "seq"), None),
        P(("dp", "seq"), None),
        P(("dp", "seq"), None),
        P(("dp", "seq"), None),
        P(("dp", "seq"), None),
        P(),
        P(),
        P(),
    )
    out_specs = (
        P("dp", "seq", None),
        P("dp", "seq", None),
        P(("dp", "seq"), None),
        P(("dp", "seq"), None),
        P(),
        P(("dp", "seq"), None),
        P(("dp", "seq"), None),
        P(),
        P(("dp", "seq"), None),
        P(("dp", "seq"), None),
        P(("dp", "seq"), None),
        P(("dp", "seq"), None),
        P(),
        P(),
    )
    return jax.shard_map(body, mesh=mesh, in_specs=in_specs, out_specs=out_specs, check_vma=False)
```

```python
import jax
import jax.numpy as jnp
from jax import lax
from jax.experimental import pallas as pl
from jax.experimental.pallas import tpu as pltpu
from jax.sharding import PartitionSpec as P

D = 1024
DI = 2048
H = 32
P_SIZE = 64
N = 128
KW = 4
STRETCH = 256
STEP = 10
CONV = 2304


norm_eps = 1e-05
beta_one = 0.9
beta_two = 0.95
learn_rate = 0.03
decay_rate = 0.1
adam_eps = 1e-08
top_precision = lax.Precision.HIGHEST


def input_norm(inputs, gain):
    scale = lax.rsqrt(jnp.mean(inputs * inputs, axis=-1, keepdims=True) + norm_eps)
    return inputs * scale * gain[None, :]


def adamw_update(param, grad, first, second):
    first_new = beta_one * first + (1.0 - beta_one) * grad
    second_new = beta_two * second + (1.0 - beta_two) * grad * grad
    corrected = first_new / (1.0 - beta_one**STEP)
    scaled = jnp.sqrt(second_new / (1.0 - beta_two**STEP)) + adam_eps
    return (
        param * (1.0 - learn_rate * decay_rate) - learn_rate * corrected / scaled,
        first_new,
        second_new,
    )


CHUNK = 128
LANES = 128
bf16 = jnp.bfloat16
f32 = jnp.float32


def contract(a, b, left, right):
    return lax.dot_general(a, b, (((left,), (right,)), ((), ())), preferred_element_type=f32)


def spread_heads(table, heads, length):
    return jnp.concatenate(
        [jnp.broadcast_to(table[:, k : k + 1], (length, P_SIZE)) for k in range(heads)], axis=1
    )


def head_slice(block, k):
    return block[:, k * P_SIZE : (k + 1) * P_SIZE]


def chunk_terms(mixed_ref, raw_ref, meta_ref, ids_ref, small_ref, width):
    length = raw_ref.shape[0]
    values = mixed_ref[:, :width].astype(f32)
    input_map = mixed_ref[:, width : width + N]
    output_map = mixed_ref[:, width + N :]
    shifted_raw = raw_ref[...] + small_ref[0:1, :]
    step_size = jnp.maximum(shifted_raw, 0.0) + jnp.log1p(jnp.exp(-jnp.abs(shifted_raw)))
    rate = -jnp.exp(small_ref[1:2, :])
    log_decay = rate * step_size
    rows_index = lax.broadcasted_iota(jnp.int32, (length, length), 0)
    cols_index = lax.broadcasted_iota(jnp.int32, (length, length), 1)
    lower = rows_index >= cols_index
    cumulative = jnp.dot(
        lower.astype(f32), log_decay, precision=top_precision, preferred_element_type=f32
    )
    flipped = cumulative.T
    same = meta_ref[:, 0:1] == ids_ref[...]
    related = same & lower
    reach = meta_ref[:, 1:2] * jnp.exp(cumulative)
    tail = meta_ref[:, 2:3] * jnp.exp(cumulative[length - 1 :, :] - cumulative)
    scores = contract(output_map, input_map, 1, 1)

    def decay_of(k):
        spans = cumulative[:, k : k + 1] - flipped[k : k + 1, :]
        return jnp.exp(jnp.where(related, spans, -1e30))

    return (values, input_map, output_map, shifted_raw, step_size, rate, log_decay, same,
            rows_index, cols_index, reach, tail, scores, decay_of)


MESH = pl.DeviceIdType.MESH
in_vmem = pl.BlockSpec(memory_space=pltpu.VMEM)


def beyond(axis, distance):
    count = lax.axis_size(axis)
    return lax.rem(lax.axis_index(axis) + distance + count, count)


def push(source, target, send_sem, recv_sem, axis, peer):
    return pltpu.make_async_remote_copy(
        src_ref=source, dst_ref=target, send_sem=send_sem, recv_sem=recv_sem,
        device_id={axis: peer}, device_id_type=MESH,
    )


def greet_all(axes):
    barrier = pltpu.get_barrier_semaphore()
    total = 0
    for axis in axes:
        for step in range(1, lax.axis_size(axis)):
            pl.semaphore_signal(barrier, inc=1, device_id={axis: beyond(axis, step)}, device_id_type=MESH)
            total += 1
    return lambda: pl.semaphore_wait(barrier, total)


def row_gather(seq_count, rows, right_send, right_recv, left_send, left_recv, core_send, core_recv):
    here = lax.axis_index("seq")
    chips = seq_count // 2
    chip, core = here // 2, lax.rem(here, 2)
    partner = here + 1 - 2 * core

    def right(k, peer):
        slot = here - 2 * (k - 1)
        return push(rows.at[slot], rows.at[slot], right_send.at[k], right_recv.at[k], "seq", peer)

    def left(k, peer):
        slot = here + 2 * (k - 1)
        return push(rows.at[slot], rows.at[slot], left_send.at[k], left_recv.at[k], "seq", peer)

    def across(q, slot):
        return push(rows.at[slot], rows.at[slot], core_send.at[q], core_recv.at[q], "seq", partner)

    def sends_right(k):
        return (chip < chips - 1) & (chip >= k - 1)

    def sends_left(k):
        return (chip > 0) & (chip + k <= chips)

    def send(k):
        if k < chips:
            @pl.when(sends_right(k))
            def _():
                right(k, here + 2).start()

            @pl.when(sends_left(k))
            def _():
                left(k, here - 2).start()

    def begin():
        send(1)
        across(chip, here).start()

    def stage(k):
        @pl.when(chip >= k)
        def _():
            slot = here - 2 * k
            push(rows.at[slot], rows.at[slot], right_send.at[k], right_recv.at[k], "seq", partner).wait_recv()

        @pl.when(chip + k < chips)
        def _():
            slot = here + 2 * k
            push(rows.at[slot], rows.at[slot], left_send.at[k], left_recv.at[k], "seq", partner).wait_recv()

        send(k + 1)

        @pl.when(chip >= k)
        def _():
            across(chip - k, here - 2 * k).start()

        @pl.when(chip + k < chips)
        def _():
            across(chip + k, here + 2 * k).start()

    def finish():
        for q in range(chips):
            across(q, 2 * q + 1 - core).wait_recv()
            across(q, 2 * q + core).wait_send()
        for k in range(1, chips):
            @pl.when(sends_right(k))
            def _(k=k):
                right(k, here + 2).wait_send()

            @pl.when(sends_left(k))
            def _(k=k):
                left(k, here - 2).wait_send()

    return begin, stage, finish


def row_scatter(seq_count, total, from_left, from_right, to_right, to_left, right_send, right_recv, left_send, left_recv):
    here = lax.axis_index("seq")
    chips = seq_count // 2
    chip = here // 2

    def right(source, q):
        return push(source.at[q], from_left.at[q], right_send.at[q], right_recv.at[q], "seq", here + 2)

    def left(source, q):
        return push(source.at[q], from_right.at[q], left_send.at[q], left_recv.at[q], "seq", here - 2)

    def begin():
        @pl.when(chip == 0)
        def _():
            for q in range(chips - 1, 0, -1):
                right(total, q).start()

        @pl.when(chip == chips - 1)
        def _():
            for q in range(chips - 1):
                left(total, q).start()

    def slot(t):
        for i in range(chips - 1):
            z = t - i
            q = chips - 1 - i
            if 1 <= z < q:
                @pl.when(chip == z)
                def _(q=q):
                    right(to_right, q).wait_recv()
                    to_right[q] = (total[q].astype(f32) + from_left[q].astype(f32)).astype(bf16)
                    right(to_right, q).start()

                @pl.when(chip == chips - 1 - z)
                def _(q=chips - 1 - q):
                    left(to_left, q).wait_recv()
                    to_left[q] = (total[q].astype(f32) + from_right[q].astype(f32)).astype(bf16)
                    left(to_left, q).start()

    def finish(acc):
        acc[...] = total[chip].astype(f32)

        @pl.when(chip > 0)
        def _():
            right(to_right, chip).wait_recv()
            acc[...] += from_left[chip].astype(f32)

        @pl.when(chip < chips - 1)
        def _():
            left(to_left, chip).wait_recv()
            acc[...] += from_right[chip].astype(f32)

        for q in range(chips):
            @pl.when(chip < q)
            def _(q=q):
                right(to_right, q).wait_send()

            @pl.when(chip > q)
            def _(q=q):
                left(to_left, q).wait_send()

    return begin, slot, finish


def scatter_scratch(block, chips):
    sems = pltpu.SemaphoreType.DMA
    return [pltpu.VMEM(block, bf16)] * 4 + [sems((chips,))] * 4


def fill_tables(seq_count, vec_ref, ids_ref, table, id_rows, small, kern, gain, skip):
    here = lax.axis_index("seq")
    width = DI // seq_count
    heads = H // seq_count
    base = D + DI
    gain[...] = vec_ref[:, pl.ds(pl.multiple_of(D + here * width, LANES), width)]
    kern[...] = jnp.zeros_like(kern)
    for k in range(KW + 1):
        start = base + k * CONV
        kern[k : k + 1, :width] = vec_ref[:, pl.ds(pl.multiple_of(start + here * width, LANES), width)]
        kern[k : k + 1, width:] = vec_ref[:, start + DI : start + CONV]
    base += (KW + 1) * CONV
    per_head = jnp.broadcast_to(vec_ref[:, base : base + 3 * H], (8, 3 * H))

    def pick(chosen):
        return jnp.dot(per_head, chosen.astype(f32), precision=top_precision, preferred_element_type=f32)

    source = lax.broadcasted_iota(jnp.int32, (3 * H, LANES), 0)
    target = lax.broadcasted_iota(jnp.int32, (3 * H, LANES), 1)
    line = lax.broadcasted_iota(jnp.int32, (8, LANES), 0)
    bias, rate = [pick((source == target + k * H + here * heads) & (target < heads)) for k in (0, 1)]
    small[...] = jnp.where(line == 0, bias, jnp.where(line == 1, rate, 0.0))
    head = lax.broadcasted_iota(jnp.int32, (3 * H, width), 0) - 2 * H - here * heads
    spot = lax.broadcasted_iota(jnp.int32, (3 * H, width), 1)
    skip[...] = pick((spot >= head * P_SIZE) & (spot < (head + 1) * P_SIZE))[0:1, :]
    ids = ids_ref[...].astype(f32)
    length = ids.shape[1]
    tall = jnp.broadcast_to(ids, (8, length))
    lane = lax.broadcasted_iota(jnp.int32, (8, length), 1)
    valid = []
    for k in range(KW - 1):
        shift = KW - 1 - k
        valid.append((pltpu.roll(tall, shift, 1) == tall) & (lane >= shift))
    none = jnp.full((1, 1), -1.0, f32)
    count = length // CHUNK
    for c in range(count):
        low, high = c * CHUNK, (c + 1) * CHUNK
        block = tall[:, low:high]
        prior = ids[:, low - 1 : low] if c else none
        after = ids[:, high : high + 1] if c + 1 < count else none
        columns = [block == prior, block == ids[:, high - 1 : high], block == after]
        columns += [v[:, low:high] for v in valid]
        merged = jnp.where(line == 0, block, 1.0)
        for k, column in enumerate(columns):
            merged = jnp.where((line == k + 1) & jnp.logical_not(column), 0.0, merged)
        table[low:high, :] = merged.T
        id_rows[c : c + 1, :] = ids[:, low:high]
    table[length:, :] = jnp.zeros((8, 8), f32)


def spread_kernel(seq_count, dp_count, in_ref, last_ref, tok_ref, vec_ref, ids_ref, out, normed, table, id_rows, small, kern, gain, skip, blocks,
                  seq_send, seq_recv, dp_send, dp_recv, right_send, right_recv, left_send, left_recv,
                  core_send, core_recv):
    here, row = lax.axis_index("seq"), lax.axis_index("dp")
    arrive = greet_all(("seq", "dp"))
    width = DI // seq_count
    heads = H // seq_count
    mixed = width + 2 * N
    chips = seq_count // 2
    shared = in_ref[:, 2 * DI : DI + CONV].astype(bf16)
    step_cols = in_ref[:, DI + CONV :].astype(bf16)
    source = lax.broadcasted_iota(jnp.int32, (H, LANES), 0)
    target = lax.broadcasted_iota(jnp.int32, (H, LANES), 1)
    for p in range(seq_count):
        own = slice(p * width, (p + 1) * width)
        blocks[p, :, :width] = in_ref[:, own].astype(bf16)
        blocks[p, :, width : 2 * width] = in_ref[:, DI + p * width : DI + (p + 1) * width].astype(bf16)
        blocks[p, :, 2 * width : width + mixed] = shared
        chosen = ((source == target + p * heads) & (target < heads)).astype(bf16)
        blocks[p, :, width + mixed : width + mixed + LANES] = contract(step_cols, chosen, 1, 0).astype(bf16)
        blocks[p, :, width + mixed + LANES :] = last_ref[:, own].astype(bf16)
    arrive()

    def seq_copy(step, peer, slot):
        return push(blocks.at[peer], out.at[row, slot], seq_send.at[step], seq_recv.at[step], "seq", peer)

    def launch(step, _):
        seq_copy(step, beyond("seq", step), here).start()
        return 0

    begin, stage, finish_rows = row_gather(seq_count, normed, right_send, right_recv, left_send, left_recv, core_send, core_recv)
    lax.fori_loop(1, seq_count, launch, 0)
    out[row, here] = blocks[here]
    normed[here] = input_norm(tok_ref[...], vec_ref[0, :D]).astype(bf16)

    quads = dp_count == 4

    def dp_copy(step, hop, from_row, source_ref):
        piece = beyond("seq", -step)
        return push(source_ref, out.at[from_row, piece], dp_send.at[step, hop], dp_recv.at[step, hop], "dp", flip(hop))

    def flip(hop):
        if not quads:
            return beyond("dp", hop)
        bit = hop if hop < 3 else 0
        low, high = lax.rem(row, 2), row // 2
        if bit == 1:
            return 2 * high + 1 - low
        return 2 * (1 - high) + low

    def origin(hop):
        if not quads:
            return beyond("dp", -hop)
        low, high = lax.rem(row, 2), row // 2
        return [row, 2 * high + 1 - low, 2 * (1 - high) + low, 3 - row][hop]

    def spread_own(step, from_blocks=False):
        piece = beyond("seq", -step)
        source_ref = blocks.at[here] if from_blocks else out.at[row, piece]
        for hop in (1, 2) if quads else range(1, dp_count):
            dp_copy(step, hop, row, source_ref).start()

    def relay_copy(step, via):
        piece = beyond("seq", -step)
        from_row = origin(via)
        return push(out.at[from_row, piece], out.at[from_row, piece], dp_send.at[step, 3], dp_recv.at[step, 3],
                    "dp", flip(3 - via))

    def relay(step):
        if not quads:
            return
        piece = beyond("seq", -step)

        for via in (1, 2):
            dp_copy(step, via, origin(via), out.at[row, piece]).wait_recv()

        @pl.when(lax.rem(step, 2) == 0)
        def _():
            relay_copy(step, 1).start()

        @pl.when(lax.rem(step, 2) == 1)
        def _():
            relay_copy(step, 2).start()

    spread_own(0, True)

    begin()
    fill_tables(seq_count, vec_ref, ids_ref, table, id_rows, small, kern, gain, skip)

    def forward(step, _):
        seq_copy(step, beyond("seq", step), beyond("seq", -step)).wait_recv()
        spread_own(step)
        relay(step - 1)
        return 0

    lax.fori_loop(1, seq_count, forward, 0)
    for k in range(1, chips):
        stage(k)
        if k == 1:
            relay(seq_count - 1)
    if chips == 1:
        relay(seq_count - 1)

    def finish(step, _):
        piece = beyond("seq", -step)
        for hop in range(1, dp_count):
            if quads and hop < 3:
                dp_copy(step, hop, row, out.at[row, piece]).wait_send()
            else:
                copy = push(out.at[row, piece], out.at[origin(hop), piece], dp_send.at[step, hop],
                            dp_recv.at[step, hop], "dp", flip(hop))
                copy.wait_recv()
                copy.wait_send()

        @pl.when(step > 0)
        def _():
            seq_copy(step, beyond("seq", step), here).wait_send()

        return 0

    lax.fori_loop(0, seq_count, finish, 0)
    finish_rows()


def spread_weights(in_weight, out_weight, inputs, vec, ids):
    seq_count, dp_count = lax.axis_size("seq"), lax.axis_size("dp")
    sems = pltpu.SemaphoreType.DMA
    width = DI // seq_count
    columns = 3 * width + 2 * N + LANES
    block = (seq_count, in_weight.shape[0], columns)
    chips = (seq_count // 2,)
    length = ids.shape[1]
    outs = shapes(
        ((dp_count,) + block, bf16), ((seq_count,) + inputs.shape, bf16), ((length + 8, 8), f32), ((length // CHUNK, CHUNK), f32),
        ((8, LANES), f32), ((8, width + 2 * N), f32), ((1, width), f32), ((1, width), f32),
    )
    scratch = [pltpu.VMEM(block, bf16)] + [sems((seq_count,))] * 2 + [sems((seq_count, dp_count))] * 2 + [sems(chips)] * 6
    return call(lambda *refs: spread_kernel(seq_count, dp_count, *refs), "spread_weights", 1, outs, scratch,
                (in_weight, out_weight, inputs, vec, ids), 0)


def rows_at(index, size):
    return pl.ds(pl.multiple_of(index * size, size), size)


def conv_window(conv_ref, c):
    return conv_ref[pl.ds(pl.multiple_of(c * CHUNK, CHUNK), CHUNK + 8), :]


def conv_before(window, table, kern_ref):
    taps = []
    total = kern_ref[KW : KW + 1, :]
    for k in range(KW):
        tap = window[8 - (KW - 1) + k : 8 - (KW - 1) + k + CHUNK, :]
        if k < KW - 1:
            tap = tap * table[:, 4 + k : 5 + k]
        taps.append(tap)
        total = total + kern_ref[k : k + 1, :] * tap
    return total, taps


def segments(count, parts):
    marks = [count * p // parts for p in range(parts + 1)]
    return list(zip(marks[:-1], marks[1:]))


def forward_kernel(seq_count, normed, weights, cotangent, table_ref, ids_ref, small_ref, kern_ref,
                   gate_ref, conv_ref, raw_ref, mixed_ref, ssd_ref, entry_ref, upstream,
                   state, *sems):
    heads = H // seq_count
    width = heads * P_SIZE
    mixed_width = width + 2 * N
    in_width = width + mixed_width + LANES
    length = normed.shape[0]
    here = lax.axis_index("seq")
    chips = seq_count // 2
    arrive = greet_all(("seq",))
    begin, stage, finish = row_gather(seq_count, upstream, *sems)
    upstream[here] = cotangent[...].astype(bf16)
    conv_ref[0:8, :] = jnp.zeros((8, mixed_width), f32)
    state[...] = jnp.zeros_like(state)
    arrive()
    begin()
    tall = 4 * CHUNK

    def project(i, _):
        out = contract(normed[rows_at(i, tall), :], weights[:, :in_width], 1, 0)
        gate_ref[rows_at(i, tall), :] = out[:, :width]
        conv_ref[pl.ds(pl.multiple_of(i * tall + 8, 8), tall), :] = out[:, width : width + mixed_width].astype(bf16).astype(f32)
        raw_ref[rows_at(i, tall), :] = out[:, width + mixed_width :]
        return 0

    lax.fori_loop(0, length // tall, project, 0)

    def chunk(c, _):
        table = table_ref[rows_at(c, CHUNK), :]
        before, _ = conv_before(conv_window(conv_ref, c), table, kern_ref)
        mixed = (before / (1.0 + jnp.exp(-before))).astype(bf16)
        mixed_ref[rows_at(c, CHUNK), :] = mixed
        (values, input_map, output_map, _, step_size, _, _, _, _, _, reach, tail, scores, decay_of) = (
            chunk_terms(mixed, raw_ref[rows_at(c, CHUNK), :], table, ids_ref[pl.ds(c, 1), :], small_ref, width)
        )
        entry = state[...]
        entry_low = entry.astype(bf16)
        entry_ref[c] = entry_low
        fed = (values * spread_heads(step_size, heads, CHUNK)).astype(bf16)
        inside = []
        for k in range(heads):
            mixing = (scores * decay_of(k)).astype(bf16)
            inside.append(contract(mixing, head_slice(fed, k), 1, 0))
        wide_reach = spread_heads(reach, heads, CHUNK)
        ssd_ref[rows_at(c, CHUNK), :] = jnp.concatenate(inside, axis=1) + wide_reach * contract(output_map, entry_low, 1, 0)
        weighted = (fed.astype(f32) * spread_heads(tail, heads, CHUNK)).astype(bf16)
        state[...] = entry * wide_reach[CHUNK - 1 :, :] + contract(input_map, weighted, 0, 0)
        return 0

    parts = segments(length // CHUNK, max(chips - 1, 1))
    for k, (low, high) in enumerate(parts):
        if k + 1 < chips:
            stage(k + 1)
        lax.fori_loop(low, high, chunk, 0)
    finish()


def shapes(*pairs):
    return [jax.ShapeDtypeStruct(shape, kind) for shape, kind in pairs]


def call(kernel, name, number, outs, scratch, operands, flops):
    params = dict(has_side_effects=True, collective_id=number, vmem_limit_bytes=60 * 1024 * 1024)
    return pl.pallas_call(
        kernel,
        out_shape=outs,
        in_specs=[in_vmem] * len(operands),
        out_specs=[in_vmem] * len(outs),
        scratch_shapes=scratch,
        compiler_params=pltpu.CompilerParams(**params),
        cost_estimate=pl.CostEstimate(flops=flops, bytes_accessed=8 * 1024 * 1024, transcendentals=0),
        name=name,
    )(*operands)


def forward(normed, weights, cotangent, table, ids, small, kern):
    seq_count = lax.axis_size("seq")
    length = normed.shape[0]
    width = DI // seq_count
    mixed_width = width + 2 * N
    count = length // CHUNK
    sems = pltpu.SemaphoreType.DMA
    outs = shapes(
        ((length, width), f32), ((length + 8, mixed_width), f32), ((length, LANES), f32), ((length, mixed_width), bf16),
        ((length, width), f32), ((count, N, width), bf16), ((seq_count,) + cotangent.shape, bf16),
    )
    scratch = [pltpu.VMEM((N, width), f32)] + [sems((seq_count // 2,))] * 6
    return call(lambda *refs: forward_kernel(seq_count, *refs), "forward", 2, outs, scratch,
                (normed, weights, cotangent, table, ids, small, kern), 2 * length * D * weights.shape[1])


def trade(term, total, theirs, got, send, recv, partner):
    block = 2 * CHUNK
    blocks = D // block

    def move(b):
        at = rows_at(b, block)
        return push(theirs.at[:, :, at], got.at[:, :, at], send.at[b], recv.at[b], "seq", partner)

    def give(b, _):
        theirs[:, :, rows_at(b, block)] = term(0, b).astype(bf16)

        @pl.when(b > 0)
        def _():
            move(b - 1).start()

        return 0

    lax.fori_loop(0, blocks, give, 0)

    def keep(b, _):
        own = term(1, b)

        @pl.when(b == 0)
        def _():
            move(blocks - 1).start()

        move(b).wait_recv()
        at = rows_at(b, block)
        total[:, :, at] = (own + got[:, :, at].astype(f32)).astype(bf16)
        return 0

    lax.fori_loop(0, blocks, keep, 0)

    def sent(b, _):
        move(b).wait_send()
        return 0

    lax.fori_loop(0, blocks, sent, 0)


def middle_kernel(seq_count, upstream, weights, ssd_ref, mixed_ref, gate_ref, gain_ref, skip_ref, normed,
                  total, grad_ref, low_ref, early, scale_ref, gain_grad, norm_row,
                  product_ref, gg_ref, part, arrived, theirs, got, out_low, sorted_ref, send, recv, stat_send, stat_recv):
    width = DI // seq_count
    here = lax.axis_index("seq")
    chips = seq_count // 2
    core = lax.rem(here, 2)
    partner = here + 1 - 2 * core
    length = upstream.shape[0]
    count = length // CHUNK
    first = weights.shape[1] - width
    tall = 4 * CHUNK
    block = 2 * CHUNK
    arrive = greet_all(("seq",))
    part[...] = jnp.zeros_like(part)
    line = lax.broadcasted_iota(jnp.int32, (2 * count, width), 0)

    def forward_part(i, _):
        at = rows_at(i, tall)
        gg = contract(upstream[at, :], weights[:, first:], 1, 0)
        gate_in = gate_ref[at, :]
        gate_act = gate_in / (1.0 + jnp.exp(-gate_in))
        product = (ssd_ref[at, :] + skip_ref[...] * mixed_ref[at, :width].astype(f32)) * gate_act
        product_ref[at, :] = product
        gg_ref[at, :] = gg
        square = product * product
        crossed = gg * gain_ref[...] * product
        sums = part[...]
        for half in range(4):
            rows = slice(half * CHUNK, (half + 1) * CHUNK)
            for offset, value in ((0, square), (count, crossed)):
                chosen = (line == 4 * i + half + offset).astype(f32)
                sums = sums + lax.dot_general(chosen, value[rows], (((1,), (1,)), ((), ())), precision=top_precision, preferred_element_type=f32)
        part[...] = sums
        return 0

    lax.fori_loop(0, length // tall, forward_part, 0)
    arrive()
    copies = [
        push(part, arrived.at[step], stat_send.at[step], stat_recv.at[step], "seq", beyond("seq", step))
        for step in range(1, seq_count)
    ]
    for copy in copies:
        copy.start()
    arrived[0] = part[...]
    long = total.shape[1]

    for j in range(chips):
        for side, piece in ((0, 2 * j + 1 - core), (1, 2 * j + core)):
            sorted_ref[side, j * long : (j + 1) * long, :] = (product_ref[rows_at(piece, long), :] * gain_ref[...]).astype(bf16)

    def term(side, b):
        return contract(sorted_ref[side], weights[rows_at(b, block), first:], 1, 1).reshape(chips, long, block)

    trade(term, total, theirs, got, send, recv, partner)
    for copy in copies:
        copy.wait_recv()
    final = arrived[here]
    for origin in range(1, seq_count):
        final = final + arrived[lax.rem(here - origin + seq_count, seq_count)]
    scale = lax.rsqrt(final[:count] / DI + norm_eps)
    pull = scale * scale * scale * final[count:] / DI
    columns = jnp.concatenate([scale, pull], axis=0).T
    lane = lax.broadcasted_iota(jnp.int32, columns.shape, 1)
    scale_ref[...] = jnp.broadcast_to(
        jnp.sum(jnp.where(lane == here, columns, 0.0), axis=1, keepdims=True), scale_ref.shape
    )
    gain_grad[...] = jnp.zeros_like(gain_grad)

    def back(j, _):
        at = rows_at(j, CHUNK)
        own_scale = jnp.sum(jnp.where(lane == j, columns, 0.0), axis=1, keepdims=True)
        own_pull = jnp.sum(jnp.where(lane == j + count, columns, 0.0), axis=1, keepdims=True)
        gate_in = gate_ref[at, :]
        gate_sig = 1.0 / (1.0 + jnp.exp(-gate_in))
        ssd_out = ssd_ref[at, :] + skip_ref[...] * mixed_ref[at, :width].astype(f32)
        product = product_ref[at, :]
        gg = gg_ref[at, :]
        grad_product = gg * gain_ref[...] * own_scale - product * own_pull
        grad_ref[at, :] = grad_product * gate_in * gate_sig
        low_ref[at, :] = (grad_product * ssd_out * (gate_sig * (1.0 + gate_in * (1.0 - gate_sig)))).astype(bf16)
        gain_grad[0:1, :] += jnp.sum(gg * product * own_scale, axis=0, keepdims=True)
        raw_out = (product * gain_ref[...]).astype(bf16).astype(f32)
        out_low[at, :] = (raw_out * own_scale).astype(bf16)
        return 0

    lax.fori_loop(0, count, back, 0)

    def weigh(b, _):
        at = rows_at(b, tall)
        gate_grad = contract(normed[:, at], low_ref[...], 0, 0)
        early[at, :width] = gate_grad.astype(bf16)
        early[at, width:] = contract(upstream[:, at], out_low[...], 0, 0).astype(bf16)
        norm_row[:, at] = row_sums(weights[at, :width].astype(f32) * gate_grad)
        return 0

    lax.fori_loop(0, D // tall, weigh, 0)
    for copy in copies:
        copy.wait_send()


def row_sums(matrix):
    ones = jnp.ones((8, matrix.shape[1]), f32)
    return lax.dot_general(ones, matrix, (((1,), (1,)), ((), ())), precision=top_precision, preferred_element_type=f32)


def middle(upstream, weights, ssd, mixed, gate_in, gain, skip, normed):
    seq_count = lax.axis_size("seq")
    length = upstream.shape[0]
    width = DI // seq_count
    chips = seq_count // 2
    count = length // CHUNK
    block = (chips, length // seq_count, D)
    sems = pltpu.SemaphoreType.DMA
    outs = shapes(
        (block, bf16), ((length, width), f32), ((length, width), bf16), ((D, 2 * width), bf16),
        ((length // seq_count, LANES), f32), ((8, width), f32), ((8, D), f32),
    )
    scratch = [
        pltpu.VMEM((length, width), f32), pltpu.VMEM((length, width), f32), pltpu.VMEM((2 * count, CHUNK), f32),
        pltpu.VMEM((seq_count, 2 * count, CHUNK), f32), pltpu.VMEM(block, bf16), pltpu.VMEM(block, bf16),
        pltpu.VMEM((length, width), bf16), pltpu.VMEM((2, length // 2, width), bf16),
        sems((D // (2 * CHUNK),)), sems((D // (2 * CHUNK),)), sems((seq_count,)), sems((seq_count,)),
    ]
    return call(lambda *refs: middle_kernel(seq_count, *refs), "middle", 4, outs, scratch,
                (upstream, weights, ssd, mixed, gate_in, gain, skip, normed), 8 * length * D * width)


def backward_kernel(seq_count, dp_count, mixed_ref, raw_ref, table_ref, ids_ref, small_ref, skip_ref, ssd_ref, entry_ref,
                    grad_ref, conv_ref, kern_ref, out_total, early, scale_ref, tok_ref,
                    late_ref, totals_ref, gkern_ref, early_sum, out_ref,
                    later, carry, ahead, acc, early_got, early_send, early_recv, *chain):
    heads = H // seq_count
    width = heads * P_SIZE
    mixed_width = width + 2 * N
    length = raw_ref.shape[0]
    count = length // CHUNK
    chips = seq_count // 2
    row = lax.axis_index("dp")
    arrive = greet_all(("seq", "dp"))
    begin, slot, finish = row_scatter(seq_count, out_total, *chain)
    for ref in (later, carry, ahead, totals_ref, gkern_ref):
        ref[...] = jnp.zeros_like(ref)
    arrive()
    begin()

    def early_copy(hop):
        peer = beyond("dp", hop)
        return push(early.at[peer], early_got.at[hop], early_send.at[hop], early_recv.at[hop], "dp", peer)

    for hop in range(1, dp_count):
        early_copy(hop).start()
    channel = lax.broadcasted_iota(jnp.int32, (width, LANES), 0)
    lane = lax.broadcasted_iota(jnp.int32, (width, LANES), 1)
    member = ((channel >= lane * P_SIZE) & (channel < (lane + 1) * P_SIZE)).astype(f32)

    def per_head(wide):
        return jnp.dot(wide, member, precision=top_precision, preferred_element_type=f32)

    def chunk(turn, _):
        c = count - 1 - turn
        at = rows_at(c, CHUNK)
        table = table_ref[at, :]
        (values, input_map, output_map, shifted_raw, step_size, rate, log_decay, same, rows_index,
         cols_index, reach, tail, scores, decay_of) = chunk_terms(
            mixed_ref[at, :], raw_ref[at, :], table, ids_ref[pl.ds(c, 1), :], small_ref, width
        )
        grad = grad_ref[at, :]
        grad_low = grad.astype(bf16)
        wide_step = spread_heads(step_size, heads, CHUNK)
        wide_reach = spread_heads(reach, heads, CHUNK)
        wide_tail = spread_heads(tail, heads, CHUNK)
        fed = (values * wide_step).astype(bf16)
        fed_full = fed.astype(f32)
        after = later[...]
        after_low = after.astype(bf16)
        grad_scores = jnp.zeros((CHUNK, CHUNK), f32)
        pieces = []
        for k in range(heads):
            decay = decay_of(k)
            mixing = (scores * decay).astype(bf16)
            own_grad = head_slice(grad_low, k)
            grad_scores = grad_scores + contract(own_grad, head_slice(fed, k), 1, 1) * decay
            pieces.append(contract(mixing, own_grad, 0, 0))
        grad_fed = jnp.concatenate(pieces, axis=1) + wide_tail * contract(input_map, after_low, 1, 0)
        reached = (grad * wide_reach).astype(bf16)
        weighted = (fed_full * wide_tail).astype(bf16)
        scores_low = grad_scores.astype(bf16)
        grad_mixed = jnp.concatenate(
            [
                wide_step * grad_fed + skip_ref[...] * grad,
                contract(scores_low, output_map, 0, 0) + contract(weighted, after_low, 1, 1),
                contract(scores_low, input_map, 1, 0) + contract(reached, entry_ref[c], 1, 1),
            ],
            axis=1,
        )
        later[...] = after * wide_reach[CHUNK - 1 :, :] + contract(output_map, reached, 0, 0)
        balance = per_head(grad_low.astype(f32) * ssd_ref[at, :] - fed_full * grad_fed)
        grad_step = per_head(values * grad_fed)
        skip_total = per_head(jnp.broadcast_to(jnp.sum(values * grad, axis=0, keepdims=True), (8, width)))
        following = (same & (rows_index <= cols_index)).astype(f32)
        grad_log = jnp.dot(
            following, balance, precision=top_precision, preferred_element_type=f32
        ) + table[:, 3:4] * carry[0:1, :]
        carry[0:1, :] = grad_log[0:1, :]
        grad_step = grad_step + rate * grad_log
        grad_raw = grad_step * jax.nn.sigmoid(shifted_raw)
        totals_ref[0:1, :] += jnp.sum(grad_raw, axis=0, keepdims=True)
        totals_ref[1:2, :] += jnp.sum(grad_log * log_decay, axis=0, keepdims=True)
        totals_ref[2:3, :] += skip_total[0:1, :]
        before, taps = conv_before(conv_window(conv_ref, c), table, kern_ref)
        sig = 1.0 / (1.0 + jnp.exp(-before))
        grad_before = grad_mixed * (sig * (1.0 + before * (1.0 - sig)))
        for k in range(KW):
            gkern_ref[k : k + 1, :] += jnp.sum(grad_before * taps[k], axis=0, keepdims=True)
        gkern_ref[KW : KW + 1, :] += jnp.sum(grad_before, axis=0, keepdims=True)
        window = jnp.concatenate([grad_before, ahead[...]], axis=0)
        ahead[...] = grad_before[:8, :]
        wide_table = table_ref[pl.ds(pl.multiple_of(c * CHUNK, CHUNK), CHUNK + 8), :]
        grad_conv = kern_ref[KW - 1 : KW, :] * grad_before
        for k in range(KW - 1):
            shift = KW - 1 - k
            masked = window * wide_table[:, 4 + k : 5 + k]
            grad_conv = grad_conv + kern_ref[k : k + 1, :] * masked[shift : shift + CHUNK, :]
        late_ref[at, :mixed_width] = grad_conv.astype(bf16)
        late_ref[at, mixed_width:] = grad_raw.astype(bf16)
        return 0

    parts = segments(count, chips - 1) if chips > 1 else [(0, count)]
    for t, (low, high) in enumerate(parts):
        lax.fori_loop(low, high, chunk, 0)
        if t + 1 < chips - 1:
            slot(t + 1)
    for hop in range(1, dp_count):
        early_copy(hop).wait_recv()

    def combine(piece, _):
        value = early[row, piece].astype(f32)
        for hop in range(1, dp_count):
            value = value + early_got[hop, piece].astype(f32)
        early_sum[piece] = value.astype(bf16)
        return 0

    lax.fori_loop(0, seq_count, combine, 0)
    finish(acc)
    out_ref[...] = tok_ref[...] + acc[...] * scale_ref[:, 0:1]
    for hop in range(1, dp_count):
        early_copy(hop).wait_send()


def backward(mixed, raw, table, ids, small, skip, ssd, entries, grad, conv_in, kern, out_total, early, scale, tokens):
    seq_count, dp_count = lax.axis_size("seq"), lax.axis_size("dp")
    length = raw.shape[0]
    width = DI // seq_count
    mixed_width = width + 2 * N
    sems = pltpu.SemaphoreType.DMA
    outs = shapes(
        ((length, mixed_width + LANES), bf16), ((8, LANES), f32), ((8, mixed_width), f32),
        (early.shape[1:], bf16), (tokens.shape, f32),
    )
    scratch = [
        pltpu.VMEM((N, width), f32), pltpu.VMEM((8, LANES), f32), pltpu.VMEM((8, mixed_width), f32), pltpu.VMEM(tokens.shape, f32),
        pltpu.VMEM(early.shape, bf16), sems((dp_count,)), sems((dp_count,)),
    ] + scatter_scratch(out_total.shape, seq_count // 2)
    return call(lambda *refs: backward_kernel(seq_count, dp_count, *refs), "backward", 5, outs, scratch,
                (mixed, raw, table, ids, small, skip, ssd, entries, grad, conv_in, kern, out_total, early, scale, tokens),
                16 * length * N * width)


def final_kernel(seq_count, dp_count, lines, low_ref, late_ref, weights, normed, early, gain_ref, norm_row, gain_grad,
                 gkern_ref, totals_ref, tok_ref, cot_ref,
                 returned, returned_early, vec_out, in_grad_ref,
                 total, theirs, got_rows, sorted_ref, part, got, summed, vec, vec_dp, vec_row, vec_seq, acc,
                 pair_send, pair_recv, dp_send, dp_recv, seq_send, seq_recv, early_send, early_recv,
                 va_send, va_recv, vb_send, vb_recv, vc_send, vc_recv, vd_send, vd_recv, *chain):
    here, row = lax.axis_index("seq"), lax.axis_index("dp")
    heads = H // seq_count
    width = DI // seq_count
    mixed_width = width + 2 * N
    in_width = width + mixed_width + LANES
    chips = seq_count // 2
    core = lax.rem(here, 2)
    partner = here + 1 - 2 * core
    hops = range(1, dp_count)
    steps = range(1, seq_count)
    tall = 4 * CHUNK
    share = part.shape[1]
    begin, slot, finish_rows = row_scatter(seq_count, total, *chain)
    arrive = greet_all(("seq", "dp"))
    arrive()

    def early_copy(step, place):
        piece = beyond("seq", step)
        return push(early.at[piece], returned_early.at[place], early_send.at[step], early_recv.at[step], "seq", piece)

    for step in steps:
        early_copy(step, here).start()
    returned_early[here] = early[here]

    long = total.shape[1]

    for j in range(chips):
        for side, piece in ((0, 2 * j + 1 - core), (1, 2 * j + core)):
            sorted_ref[side, j * long : (j + 1) * long, :width] = low_ref[rows_at(piece, long), :]
            sorted_ref[side, j * long : (j + 1) * long, width:] = late_ref[rows_at(piece, long), :]

    def term(side, b):
        return contract(sorted_ref[side], weights[rows_at(b, 2 * CHUNK), :in_width], 1, 1).reshape(chips, long, 2 * CHUNK)

    trade(term, total, theirs, got_rows, pair_send, pair_recv, partner)
    begin()

    vec[...] = jnp.zeros_like(vec)

    def weigh(b, _):
        at = rows_at(b, tall)
        grads = contract(normed[:, at], late_ref[...], 0, 0)
        for i in range(tall // share):
            part[b * (tall // share) + i] = grads[i * share : (i + 1) * share, :].astype(bf16)
        sums = row_sums(weights[at, width:in_width].astype(f32) * grads)
        sums = (sums + norm_row[:, at]) / gain_ref[:, at]
        for j in range(tall // LANES):
            vec[pl.ds(b * (tall // LANES) + j, 1), :] = sums[0:1, j * LANES : (j + 1) * LANES]
        return 0

    lax.fori_loop(0, D // tall, weigh, 0)

    def write(base, source, line, columns, moving):
        for j in range(columns[0] // LANES, columns[1] // LANES):
            at = base + j - columns[0] // LANES
            if moving:
                at = at + here * (width // LANES)
            vec[pl.ds(at, 1), :] = source[line : line + 1, j * LANES : (j + 1) * LANES]

    base = D // LANES
    write(base, gain_grad, 0, (0, width), True)
    base += DI // LANES
    for k in range(KW + 1):
        write(base, gkern_ref, k, (0, width), True)
        write(base + DI // LANES, gkern_ref, k, (width, mixed_width), False)
        base += CONV // LANES
    source = lax.broadcasted_iota(jnp.int32, (LANES, LANES), 0)
    target = lax.broadcasted_iota(jnp.int32, (LANES, LANES), 1)
    tail = jnp.zeros((8, LANES), f32)
    picked = lax.broadcasted_iota(jnp.int32, (8, LANES), 0)
    sums = totals_ref[...]
    for k in range(3):
        chosen = ((target == source + k * H + here * heads) & (source < heads)).astype(f32)
        tail = tail + jnp.dot(jnp.where(picked == k, sums, 0.0), chosen, precision=top_precision, preferred_element_type=f32)
    vec[base : base + 1, :] = jnp.sum(tail, axis=0, keepdims=True)

    wide = seq_count * lines
    first = [push(vec.at[rows_at(beyond("dp", hop), wide), :], vec_dp.at[hop], va_send.at[hop], va_recv.at[hop], "dp", beyond("dp", hop)) for hop in hops]
    for copy in first:
        copy.start()
    def dp_copy(step, hop):
        piece = beyond("seq", step)
        peer = beyond("dp", hop)
        return push(part.at[peer * seq_count + piece], got.at[hop, piece], dp_send.at[step, hop], dp_recv.at[step, hop], "dp", peer)

    def launch(step, _):
        for hop in hops:
            dp_copy(lax.rem(step, seq_count), hop).start()
        return 0

    lax.fori_loop(1, seq_count + 1, launch, 0)
    for copy in first:
        copy.wait_recv()
    value = vec[rows_at(row, wide), :]
    for hop in hops:
        value = value + vec_dp[hop]
    vec_row[...] = value
    second = [push(vec_row.at[rows_at(beyond("seq", step), lines), :], vec_seq.at[step], vb_send.at[step], vb_recv.at[step], "seq", beyond("seq", step)) for step in steps]
    for copy in second:
        copy.start()
    if chips > 2:
        slot(1)

    def seq_copy(step, place):
        piece = beyond("seq", step)
        return push(summed.at[piece], returned.at[place], seq_send.at[step], seq_recv.at[step], "seq", piece)

    def combined(step):
        piece = beyond("seq", step)
        for hop in hops:
            dp_copy(step, hop).wait_recv()
        value = part[row * seq_count + piece].astype(f32)
        for hop in hops:
            value = value + got[hop, piece].astype(f32)
        return value.astype(bf16)

    def swap(step, _):
        summed[beyond("seq", step)] = combined(step)
        seq_copy(step, here).start()
        return 0

    half = seq_count // 2
    lax.fori_loop(1, half, swap, 0)
    for t in range(2, chips - 1):
        slot(t)
    for copy in second:
        copy.wait_recv()
    final = vec_row[rows_at(here, lines), :]
    for step in steps:
        final = final + vec_seq[step]
    spot = row * seq_count + here
    vec_out[rows_at(spot, lines), :] = final

    def third(step, place):
        at = rows_at(row * seq_count + place, lines)
        return push(vec_out.at[rows_at(spot, lines), :], vec_out.at[at, :], vc_send.at[step], vc_recv.at[step], "seq", beyond("seq", step))

    for step in steps:
        third(step, here).start()
    lax.fori_loop(half, seq_count, swap, 0)
    returned[here] = combined(0)
    for step in steps:
        third(step, beyond("seq", -step)).wait_recv()

    def fourth(hop, place):
        return push(vec_out.at[rows_at(row, wide), :], vec_out.at[rows_at(place, wide), :], vd_send.at[hop], vd_recv.at[hop], "dp", beyond("dp", hop))

    for hop in hops:
        fourth(hop, row).start()
    finish_rows(acc)
    inputs = tok_ref[...]
    scale = lax.rsqrt(jnp.mean(inputs * inputs, axis=-1, keepdims=True) + norm_eps)
    pulled = acc[...] * gain_ref[:, :D]
    dots = jnp.sum(pulled * inputs, axis=-1, keepdims=True)
    in_grad_ref[...] = cot_ref[...] + scale * pulled - inputs * (scale * scale * scale * dots / D)

    def close(step, _):
        seq_copy(step, beyond("seq", -step)).wait_recv()
        seq_copy(step, here).wait_send()
        early_copy(step, beyond("seq", -step)).wait_recv()
        early_copy(step, here).wait_send()
        return 0

    lax.fori_loop(1, seq_count, close, 0)

    def drain(step, _):
        for hop in hops:
            dp_copy(step, hop).wait_send()
        return 0

    lax.fori_loop(0, seq_count, drain, 0)
    for hop in hops:
        fourth(hop, beyond("dp", -hop)).wait_recv()
        fourth(hop, row).wait_send()
    for copy in first + second:
        copy.wait_send()
    for step in steps:
        third(step, here).wait_send()


def final(low, late, weights, normed, early, gain, norm_row, gain_grad, gkern, totals, tokens, cotangent):
    seq_count, dp_count = lax.axis_size("seq"), lax.axis_size("dp")
    devices = seq_count * dp_count
    chips = seq_count // 2
    vec_size = D + DI + (KW + 1) * CONV + 3 * H
    lines = -(-vec_size // (devices * LANES * 8)) * 8
    share = D // devices
    columns = late.shape[1]
    block = (chips,) + tokens.shape
    sems = pltpu.SemaphoreType.DMA
    outs = shapes(
        ((seq_count, share, columns), bf16), (early.shape, bf16), ((devices * lines, LANES), f32), (tokens.shape, f32)
    )
    scratch = [
        pltpu.VMEM(block, bf16), pltpu.VMEM(block, bf16), pltpu.VMEM(block, bf16),
        pltpu.VMEM((2, late.shape[0] // 2, low.shape[1] + columns), bf16), pltpu.VMEM((devices, share, columns), bf16),
        pltpu.VMEM((dp_count, seq_count, share, columns), bf16), pltpu.VMEM((seq_count, share, columns), bf16),
        pltpu.VMEM((devices * lines, LANES), f32), pltpu.VMEM((dp_count, seq_count * lines, LANES), f32),
        pltpu.VMEM((seq_count * lines, LANES), f32), pltpu.VMEM((seq_count, lines, LANES), f32), pltpu.VMEM(tokens.shape, f32),
    ]
    counts = [(D // (2 * CHUNK),)] * 2 + [(seq_count, dp_count)] * 2 + [(seq_count,)] * 4 + [(dp_count,)] * 2 + [(seq_count,)] * 4 + [(dp_count,)] * 2
    scratch += [sems(shape) for shape in counts] + scatter_scratch(block, chips)
    return call(lambda *refs: final_kernel(seq_count, dp_count, lines, *refs), "final", 3, outs, scratch,
                (low, late, weights, normed, early, gain, norm_row, gain_grad, gkern, totals, tokens, cotangent),
                4 * D * D * columns)


def body(tokens, cotangent, doc_ids, in_weight, out_weight, in_m, in_v, out_m, out_v, vec_params, vec_m, vec_v):
    seq_count = lax.axis_size("seq")
    heads = H // seq_count
    width = DI // seq_count
    mixed_width = width + 2 * N
    owner_rows = in_weight.shape[0]
    inputs = tokens[0]
    upstream_f = cotangent[0]

    vec = vec_params[None, :]
    weights, normed_all, table, ids_rows, small, kern, own_gain, wide_skip = spread_weights(
        in_weight, out_weight, inputs, vec, doc_ids
    )
    weights = weights.reshape(D, -1)
    normed_all = normed_all.reshape(-1, D)
    gate_in, conv_in, raw, mixed, ssd, entries, upstream_all = forward(
        normed_all, weights, upstream_f, table, ids_rows, small, kern
    )
    upstream_all = upstream_all.reshape(-1, D)
    out_total, grad_ssd, gate_low, early, scale, gain_grad, norm_row = middle(
        upstream_all, weights, ssd, mixed, gate_in, own_gain, wide_skip, normed_all
    )
    early = early.reshape(lax.axis_size("dp"), seq_count, owner_rows, -1)
    late, totals, gkern, early, outputs = backward(
        mixed, raw, table, ids_rows, small, wide_skip, ssd, entries, grad_ssd, conv_in, kern, out_total, early, scale, inputs
    )
    returned, returned_early, vec_sum, input_grad = final(
        gate_low, late, weights, normed_all, early, vec, norm_row, gain_grad, gkern, totals, inputs, upstream_f
    )
    returned = returned.astype(f32)
    returned_early = returned_early.astype(f32)
    vec_grad = vec_sum.reshape(-1)[: vec_params.shape[0]]

    def gathered(array, start, size):
        return array[:, :, start : start + size].transpose(1, 0, 2).reshape(owner_rows, -1)

    in_grad = jnp.concatenate(
        [
            gathered(returned_early, 0, width),
            gathered(returned, 0, width),
            jnp.sum(returned[:, :, width : width + 2 * N], axis=0),
            gathered(returned, mixed_width, heads),
        ],
        axis=1,
    )
    out_grad = gathered(returned_early, width, width)

    in_new, in_m_new, in_v_new = adamw_update(in_weight, in_grad, in_m, in_v)
    out_new, out_m_new, out_v_new = adamw_update(out_weight, out_grad, out_m, out_v)
    vec_new, vec_m_new, vec_v_new = adamw_update(vec_params, vec_grad, vec_m, vec_v)
    return (
        outputs[None],
        input_grad[None],
        in_grad,
        out_grad,
        vec_grad,
        in_new,
        out_new,
        vec_new,
        in_m_new,
        in_v_new,
        out_m_new,
        out_v_new,
        vec_m_new,
        vec_v_new,
    )


def solution(mesh):
    in_specs = (
        P("dp", "seq", None),
        P("dp", "seq", None),
        P("dp", None),
        P(("dp", "seq"), None),
        P(("dp", "seq"), None),
        P(("dp", "seq"), None),
        P(("dp", "seq"), None),
        P(("dp", "seq"), None),
        P(("dp", "seq"), None),
        P(),
        P(),
        P(),
    )
    out_specs = (
        P("dp", "seq", None),
        P("dp", "seq", None),
        P(("dp", "seq"), None),
        P(("dp", "seq"), None),
        P(),
        P(("dp", "seq"), None),
        P(("dp", "seq"), None),
        P(),
        P(("dp", "seq"), None),
        P(("dp", "seq"), None),
        P(("dp", "seq"), None),
        P(("dp", "seq"), None),
        P(),
        P(),
    )
    return jax.shard_map(body, mesh=mesh, in_specs=in_specs, out_specs=out_specs, check_vma=False)
```
